256 devices in a mesh: dp: 2 (over core), space: 128 (over x, z, y).
Axes of the slice: x: 4, y: 4, z: 8, core: 2. Of those that a mesh axis runs over, the one named last changes fastest.
Arguments:
- feats: bfloat16 [262144, 64], P(('dp', 'space')), parts along dimension 0, may hold values from -6 to 6
- w_conv: bfloat16 [1728, 64], replicated, may hold values from -0.1875 to 0.1875
- w_down: bfloat16 [512, 128], replicated, may hold values from -0.375 to 0.375
- neighbors: int32 [27, 262144], P(None, ('dp', 'space')), parts along dimension 1, may hold values from 0 to 3072, as said below
- parent: int32 [262144], P(('dp', 'space')), parts along dimension 0, may hold values from 0 to 32767, as said below
- octant: int32 [262144], P(('dp', 'space')), parts along dimension 0, may hold values from 0 to 7, as said below
- grad_out: bfloat16 [65536, 128], P(('dp', 'space')), parts along dimension 0, may hold values from -6 to 6
Outputs:
- coarse_out: bfloat16 [65536, 128], P(('dp', 'space')), parts along dimension 0
- grad_feats: bfloat16 [262144, 64], P(('dp', 'space')), parts along dimension 0
- grad_conv: float32 [3456, 64], P('dp'), parts along dimension 0
- grad_down: float32 [1024, 128], P('dp'), parts along dimension 0
The draws below stay inside these ranges and needn't reach their ends.
There are 2 independent parts, one for each index of `dp`. The reference program is written for one: setup_inputs(seed, part) draws one part's arguments, and reference() takes and returns one part's arrays. A program takes and returns all parts, laid end to end along the dimension named above; an argument that names none is the same for every part. Nothing has to cross between parts.
Inputs may be any that keep to these rules, and one draw needn't show every extreme that they name: For v in aligned block j of 1024 rows, neighbors[k, v] = r < 3072 names the fine voxel (j - 1) * 1024 + r at offset (k // 9 - 1, k // 3 % 3 - 1, k % 3 - 1) from v, and 3072 marks an empty cell; neighbors[13, v] = 1024 + v % 1024; a named row of block j - 1 is among its last 512 rows and a named row of block j + 1 among its first 512 rows; rows of block 0 never name block -1 and rows of the last block never name the block after it; the table is symmetric: the voxel named by neighbors[k, v] names v at offset 26 - k. A fine voxel in aligned block j of 1024 rows has its parent in coarse block j or j - 1 of 256 rows, block 127 standing for j - 1 when j = 0; no two fine voxels share both parent and octant. `octant`: the corner of the parent's 2x2x2 cell that the fine voxel occupies.
All inputs are finite; a program needn't handle non-finite values.
Results may differ from the reference program's by a relative error of at most 0.0049.
Values may be sent and summed in bfloat16 or wider, within the bound.
A program may use at most 64 MiB of HBM per device.

```python
import math
import jax
import jax.numpy as jnp

C = 64
C2 = 128
SLAB_X = 4
SLAB_Y = 32
SLAB_Z = 16
V_DEV = 1024
VC_DEV = 256
VOXELS = 131072
COARSE = 32768
N_SPACE = 128


def geometry(key):
    base = jax.random.fold_in(key, 7)
    cells = SLAB_X * SLAB_Y * SLAB_Z
    keys = jax.random.split(base, N_SPACE)

    def pick_cells(slab_key):
        order = jax.random.permutation(slab_key, cells)
        return jnp.zeros((cells,), jnp.int32).at[order[:V_DEV]].set(1)
    occupied = jax.vmap(pick_cells)(keys)
    ranking = jnp.cumsum(occupied, axis=1) - 1
    block_base = jnp.arange(N_SPACE, dtype=jnp.int32)[:, None] * V_DEV
    ident = jnp.where(occupied == 1, block_base + ranking, VOXELS).astype(jnp.int32)
    grid = ident.reshape(N_SPACE * SLAB_X, SLAB_Y, SLAB_Z)
    padded = jnp.pad(grid, 1, constant_values=VOXELS)
    places = jnp.nonzero(occupied.reshape(-1), size=VOXELS)[0].astype(jnp.int32)
    xpos = places // (SLAB_Y * SLAB_Z)
    ypos = places // SLAB_Z % SLAB_Y
    zpos = places % SLAB_Z
    stacked = []
    for step_x in (-1, 0, 1):
        for step_y in (-1, 0, 1):
            for step_z in (-1, 0, 1):
                stacked.append(padded[xpos + 1 + step_x, ypos + 1 + step_y, zpos + 1 + step_z])
    global_table = jnp.stack(stacked, axis=0).astype(jnp.int32)
    row_base = ((jnp.arange(VOXELS, dtype=jnp.int32) // V_DEV - 1) * V_DEV).astype(jnp.int32)
    neighbor_table = jnp.where(global_table == VOXELS, 3 * V_DEV, global_table - row_base[None, :]).astype(jnp.int32)
    layer = xpos // 2
    shifted = (layer - 1) % (2 * N_SPACE)
    owner = shifted // 2
    local_layer = shifted % 2
    half_y = SLAB_Y // 2
    half_z = SLAB_Z // 2
    parent_ids = owner * VC_DEV + local_layer * half_y * half_z + ypos // 2 * half_z + zpos // 2
    corner = xpos % 2 * 4 + ypos % 2 * 2 + zpos % 2
    return (neighbor_table, parent_ids.astype(jnp.int32), corner.astype(jnp.int32))


def draw_neighbors(key, part):
    return geometry(key)[0]


def draw_parent(key, part):
    return geometry(key)[1]


def draw_octant(key, part):
    return geometry(key)[2]


def block_levels(key, shape, shards, smallest, top_value):
    factor_of, own = 1.0, jax.random.fold_in(key, 6)
    for dim, shards_of in shards:
        heights = jnp.exp(jax.random.uniform(jax.random.fold_in(own, dim), (shards_of,), jnp.float32, smallest / len(shards), top_value / len(shards)))
        factor_of = factor_of * jnp.repeat(heights, shape[dim] // shards_of).reshape([-1 if axis == dim else 1 for axis in range(len(shape))])
    return factor_of


def bell_draw(stream_key, extent, deviation, most, shards=(), held_as=jnp.bfloat16):
    level = block_levels(stream_key, extent, shards, -0.22, 0.18) if shards else 1.0
    values = jax.random.normal(stream_key, extent, jnp.float32) * deviation * level
    return jnp.minimum(jnp.maximum(values, -most), most).astype(held_as)


def setup_inputs(seed: int = 0, part: int = 0) -> dict:
    seeds = jax.random.split(jax.random.key(seed), 8)
    part_splits = jax.random.split(jax.random.fold_in(seeds[7], part), 8)
    feats = bell_draw(part_splits[0], (VOXELS, C), 1.0, 6.0, ((0, 128),))
    w_conv = bell_draw(seeds[1], (27 * C, C), (14 * C) ** -0.5, 0.1875)
    w_down = bell_draw(seeds[2], (8 * C, C2), (4 * C) ** -0.5, 0.375)
    neighbors = draw_neighbors(jax.random.fold_in(jax.random.fold_in(seeds[7], part), 71), part)
    parent = draw_parent(jax.random.fold_in(jax.random.fold_in(seeds[7], part), 71), part)
    octant = draw_octant(jax.random.fold_in(jax.random.fold_in(seeds[7], part), 71), part)
    grad_out = bell_draw(part_splits[6], (COARSE, C2), 1.0, 6.0, ((0, 128),))
    return dict(feats=feats, w_conv=w_conv, w_down=w_down, neighbors=neighbors, parent=parent, octant=octant, grad_out=grad_out)


def reference(feats, w_conv, w_down, neighbors, parent, octant, grad_out):
    voxels, channels = feats.shape
    coarse_count = grad_out.shape[0]
    block_base = ((jnp.arange(voxels, dtype=jnp.int32) // V_DEV - 1) * V_DEV).astype(jnp.int32)
    global_nbr = jnp.where(neighbors == 3 * V_DEV, voxels, neighbors + block_base[None, :]).astype(jnp.int32)
    zero_row = jnp.zeros((1, channels), jnp.bfloat16)
    lookup = jnp.concatenate([feats, zero_row], axis=0)
    preact = jnp.zeros((voxels, channels), jnp.float32)
    for offset in range(27):
        weight_block = w_conv[offset * channels:(offset + 1) * channels]
        preact = preact + jnp.dot(lookup[global_nbr[offset]], weight_block, preferred_element_type=jnp.float32)
    middle = (feats.astype(jnp.float32) + jax.nn.silu(preact)).astype(jnp.bfloat16)
    parent_grads = grad_out[parent]
    partial_value = jnp.zeros((voxels, w_down.shape[1]), jnp.float32)
    back_mid = jnp.zeros((voxels, channels), jnp.float32)
    down_blocks = []
    for octant_id in range(8):
        chosen = (octant == octant_id)[:, None]
        down_block = w_down[octant_id * channels:(octant_id + 1) * channels]
        partial_value = partial_value + jnp.where(chosen, jnp.dot(middle, down_block, preferred_element_type=jnp.float32), jnp.float32(0.0))
        back_mid = back_mid + jnp.where(chosen, jnp.dot(parent_grads, down_block.T, preferred_element_type=jnp.float32), jnp.float32(0.0))
        masked = jnp.where(chosen, middle, jnp.zeros_like(middle))
        down_blocks.append(jnp.dot(masked.T, parent_grads, preferred_element_type=jnp.float32))
    coarse_out = jax.ops.segment_sum(partial_value, parent, coarse_count).astype(jnp.bfloat16)
    grad_scale = 1.0 / math.sqrt(voxels)
    grad_down = jnp.concatenate(down_blocks, axis=0) * grad_scale
    sigmoid_pre = jax.nn.sigmoid(preact)
    grad_pre = (back_mid * sigmoid_pre * (1.0 + preact * (1.0 - sigmoid_pre))).astype(jnp.bfloat16)
    conv_blocks = []
    spilled = jnp.zeros((voxels + 1, channels), jnp.float32)
    for offset in range(27):
        weight_block = w_conv[offset * channels:(offset + 1) * channels]
        conv_blocks.append(jnp.dot(lookup[global_nbr[offset]].T, grad_pre, preferred_element_type=jnp.float32))
        terms = jnp.dot(grad_pre, weight_block.T, preferred_element_type=jnp.float32)
        spilled = spilled + jax.ops.segment_sum(terms, global_nbr[offset], voxels + 1)
    grad_conv = jnp.concatenate(conv_blocks, axis=0) * grad_scale
    grad_feats = (back_mid + spilled[:voxels]).astype(jnp.bfloat16)
    return (coarse_out, grad_feats, grad_conv, grad_down)
```

```python
import functools
import math

import jax
import jax.numpy as jnp
from jax import lax
from jax.experimental import pallas as pl
from jax.experimental.pallas import tpu as pltpu
from jax.sharding import PartitionSpec as P

F32 = jnp.float32
BF16 = jnp.bfloat16
C = 64
C2 = 128
V = 1024
HALF = 512
VC = 256
SY, SZ = 32, 16
LAYER = SY * SZ
CELLS = 4 * LAYER
WIDE = CELLS + 2 * LAYER
EMPTY = 3 * V
TAPS = 9 * C
ROWS_A, ROWS_B = 768, 640
CHIPS = {128: (4, 8, 4), 16: (2, 2, 4)}


def dot(a, b):
    return jnp.dot(a, b, preferred_element_type=F32)


def dot_nt(a, b):
    return lax.dot_general(a, b, (((1,), (1,)), ((), ())), preferred_element_type=F32)


def dot_tn(a, b):
    return lax.dot_general(a, b, (((0,), (0,)), ((), ())), preferred_element_type=F32)


def hot(rows, ids, start):
    at = lax.broadcasted_iota(jnp.int32, (rows, ids.shape[1]), 0) + start
    return jnp.where(at == ids, 1.0, 0.0).astype(BF16)


def peer(place, dims, axis, step):
    _, nz, ny = dims
    y, z, x = place % ny, place // ny % nz, place // (ny * nz)
    if axis == "y":
        return place - y + (y + step) % ny
    if axis == "z":
        return place + ((z + step) % nz - z) * ny
    return place + ((x + step) % dims[0] - x) * (ny * nz)


def greet(partners):
    barrier = pltpu.get_barrier_semaphore()
    for other in partners:
        pl.semaphore_signal(
            barrier, inc=1, device_id={"space": other}, device_id_type=pl.DeviceIdType.MESH
        )
    pl.semaphore_wait(barrier, len(partners))


def push(src, dst, send, recv, other):
    copy = pltpu.make_async_remote_copy(
        src_ref=src,
        dst_ref=dst,
        send_sem=send,
        recv_sem=recv,
        device_id={"space": other},
        device_id_type=pl.DeviceIdType.MESH,
    )
    copy.start()
    return copy


def halo_kernel(
    count, feats, table, grads, prev_f, next_f, prev_t, next_t, prev_g, send, recv
):
    place = lax.axis_index("space")
    after, before = (place + 1) % count, (place + count - 1) % count
    greet((after, before))
    copies = [
        push(feats.at[:, pl.ds(HALF, HALF)], prev_f, send.at[0], recv.at[0], after),
        push(feats.at[:, pl.ds(0, HALF)], next_f, send.at[1], recv.at[1], before),
        push(table.at[:, pl.ds(HALF, HALF)], prev_t, send.at[2], recv.at[2], after),
        push(table.at[:, pl.ds(0, HALF)], next_t, send.at[3], recv.at[3], before),
        push(grads, prev_g, send.at[4], recv.at[4], after),
    ]
    for copy in copies:
        copy.wait()


def cell_maps(table, prev_t, next_t, own_hot, prev_hot, next_hot):
    own = table[0:1, :].astype(jnp.int32)
    has_prev, has_next = table[3:4, 0:HALF], table[4:5, 0:HALF]
    prev = jnp.where(has_prev > 0.0, prev_t[0:1, :], -1.0).astype(jnp.int32)
    after = jnp.where(has_next > 0.0, next_t[0:1, :], -1.0).astype(jnp.int32)
    for start in range(0, CELLS, 256):
        own_hot[start : start + 256, :] = hot(256, own, start)
    prev_hot[...] = hot(LAYER, prev, 3 * LAYER)
    next_hot[...] = hot(LAYER, after, 0)


def edge_masks():
    lane = lax.broadcasted_iota(jnp.int32, (1, WIDE), 1)
    y, z = lane // SZ % SY, lane % SZ
    masks = []
    for dy in (-1, 0, 1):
        for dz in (-1, 0, 1):
            inside = (y + dy >= 0) & (y + dy < SY) & (z + dz >= 0) & (z + dz < SZ)
            masks.append(jnp.where(inside, 1.0, 0.0))
    return masks


def shifted(block, tap, masks):
    step = (tap // 3 - 1) * SZ + tap % 3 - 1
    if step == 0:
        return block
    return pltpu.roll(block, (-step) % WIDE, 1) * masks[tap]


def unfold(wide, masks, taps):
    for group in range(0, C, 16):
        block = wide[group : group + 16, :]
        for tap in range(9):
            taps[tap * C + group : tap * C + group + 16, :] = shifted(block, tap, masks).astype(
                BF16
            )


def fold(spread):
    return (
        spread[0:C, 0:CELLS]
        + spread[C : 2 * C, LAYER : LAYER + CELLS]
        + spread[2 * C : 3 * C, 2 * LAYER : 2 * LAYER + CELLS]
    )


def to_voxels(cells, own_hot):
    high = cells.astype(BF16)
    low = (cells - high.astype(F32)).astype(BF16)
    both = dot(jnp.concatenate([high, low], axis=0), own_hot[...])
    return both[0:C] + both[C : 2 * C]


def named_rows(names, rows, candidates):
    for start in range(0, CELLS, 256):
        rows[start : start + 256, :] = hot(256, names, start + HALF)
    return dot(candidates, rows[...]).astype(BF16)


def pieces(ids):
    high = lax.shift_right_logical(ids, 6)
    return high.astype(F32), (ids & 63).astype(F32)


def block_kernel(
    feats, prev_f, next_f, table, prev_t, next_t, nbr, w_conv, w_down, grads, prev_g,
    grad_pre, back, part_a, part_b, coarse_own, coarse_prev, flag,
    own_hot, prev_hot, next_hot, wide, taps, stack, named, preact, conv, lookup, parent_hot, spread,
):
    cell_maps(table, prev_t, next_t, own_hot, prev_hot, next_hot)
    masks = edge_masks()

    lane = lax.broadcasted_iota(jnp.int32, (1, V), 1)
    named[...] = jnp.zeros_like(named)
    named[0:27, :] = EMPTY - nbr[...]
    named[27:28, :] = 2 * V - lane
    high, low = pieces(named[...])
    own = jnp.concatenate([feats[...], high.astype(BF16), low.astype(BF16)], axis=0)
    own = dot_nt(own, own_hot[...])
    wide[0:C, LAYER : LAYER + CELLS] = own[0:C]
    told = own[C : C + 32] * 64.0 + own[C + 32 : C + 64]
    row = lax.broadcasted_iota(jnp.int32, (16, HALF), 0)
    half_lane = lax.broadcasted_iota(jnp.int32, (16, HALF), 1)
    for edge, where_hot, ids, at in (
        (prev_f, prev_hot, EMPTY - HALF - half_lane, 0),
        (next_f, next_hot, V - half_lane, LAYER + CELLS),
    ):
        high, low = pieces(ids)
        tail = jnp.where(row == 0, high, jnp.where(row == 1, low, 0.0)).astype(BF16)
        placed = dot_nt(jnp.concatenate([edge[...], tail], axis=0), where_hot[...])
        wide[0:C, at : at + LAYER] = placed[0:C]
        wide[C : C + 8, at : at + LAYER] = jnp.broadcast_to(
            placed[C : C + 1] * 64.0 + placed[C + 1 : C + 2], (8, LAYER)
        )
    wide[C : C + 8, LAYER : LAYER + CELLS] = jnp.broadcast_to(told[27:28], (8, CELLS))

    ids = wide[C : C + 8, :]
    wrong = jnp.zeros((1, CELLS), F32)
    for tap in range(9):
        seen = shifted(ids, tap, masks)[0:1]
        for layer in range(3):
            k = layer * 9 + tap
            wrong = jnp.maximum(
                wrong, jnp.abs(told[k : k + 1] - seen[:, layer * LAYER : layer * LAYER + CELLS])
            )
    wrong = jnp.max(jnp.where(told[27:28] > 0.0, wrong, 0.0))
    outside = jnp.min(table[0:1, :])
    general = jnp.logical_or(wrong > 0.0, outside < 0.0)
    flag[0] = jnp.where(general, 1, 0)

    unfold(wide, masks, taps)
    weights = jnp.concatenate(
        [w_conv[:, d * TAPS : (d + 1) * TAPS] for d in range(3)], axis=0
    )
    preact[...] = to_voxels(fold(dot(weights, taps[...])), own_hot)

    candidates = lambda: jnp.concatenate([prev_f[...], feats[...], next_f[...]], axis=1)

    @pl.when(general)
    def _():
        preact[...] = jnp.zeros_like(preact)
        rows = candidates()

        def pair(i, carry):
            block = w_conv[:, pl.ds(pl.multiple_of(i * 128, 128), 128)]
            for half in range(2):
                read = named_rows(nbr[pl.ds(2 * i + half, 1), :], own_hot, rows)
                preact[...] += dot(block[:, half * C : (half + 1) * C], read)
            return carry

        lax.fori_loop(0, 13, pair, 0)
        preact[...] += dot(w_conv[:, 26 * C : 27 * C], named_rows(nbr[26:27, :], own_hot, rows))

    act = preact[...]
    gate = jax.nn.sigmoid(act)
    middle = (feats[...].astype(F32) + act * gate).astype(BF16)

    lookup[0:VC, :] = prev_g[...]
    lookup[VC : 2 * VC, :] = grads[...]
    parent_hot[...] = hot(2 * VC, table[1:2, :].astype(jnp.int32), 0)
    parent_grads = dot_tn(lookup[...], parent_hot[...]).astype(BF16)
    back_all = dot(w_down[...], parent_grads)
    octant = table[2:3, :]
    total = jnp.zeros((C, V), F32)
    for o in range(8):
        chosen = jnp.broadcast_to(octant == float(o), (C, V))
        total += jnp.where(chosen, back_all[o * C : (o + 1) * C], 0.0)
        spread[o * C : (o + 1) * C, :] = jnp.where(chosen, middle.astype(F32), 0.0).astype(BF16)
    back[...] = total
    children = dot_nt(spread[...], parent_hot[...]).astype(BF16)
    sums = dot_tn(children, w_down[...])
    coarse_prev[...] = sums[0:VC].astype(BF16)
    coarse_own[...] = sums[VC : 2 * VC]
    part_b[128:ROWS_B, :] = dot(children, lookup[...])

    slope = (total * gate * (1.0 + act * (1.0 - gate))).astype(BF16)
    grad_pre[...] = slope

    @pl.when(jnp.logical_not(general))
    def _():
        placed = dot_nt(slope, own_hot[...]).astype(BF16)
        stack[...] = jnp.zeros_like(stack)
        for d in range(3):
            stack[d * C : (d + 1) * C, d * LAYER : d * LAYER + CELLS] = placed
        product = dot_nt(stack[...], taps[...])
        flat = jnp.concatenate([product[d * C : (d + 1) * C] for d in range(3)], axis=1)
        conv[:, 27 * C : 28 * C] = jnp.zeros((C, C), F32)
        conv[:, 0 : 27 * C] = flat

    @pl.when(general)
    def _():
        rows = candidates()
        slopes = grad_pre[...]

        def pair(i, carry):
            both = [
                dot_nt(slopes, named_rows(nbr[pl.ds(2 * i + half, 1), :], own_hot, rows))
                for half in range(2)
            ]
            conv[:, pl.ds(pl.multiple_of(i * 128, 128), 128)] = jnp.concatenate(both, axis=1)
            return carry

        lax.fori_loop(0, 13, pair, 0)
        last = dot_nt(slopes, named_rows(nbr[26:27, :], own_hot, rows))
        conv[:, 26 * C : 28 * C] = jnp.concatenate([last, jnp.zeros_like(last)], axis=1)

    for t in range(12):
        part_a[t * C : (t + 1) * C, :] = conv[:, t * 128 : (t + 1) * 128]
    for t in range(2):
        part_b[t * C : (t + 1) * C, :] = conv[:, (12 + t) * 128 : (13 + t) * 128]


def total_kernel(
    count, dims, grad_pre, coarse, part_a, part_b,
    prev_p, next_p, coarse_in, done,
    got_a1, got_b1, sum_a1, sum_b1, got_a2, got_b2, got_z,
    halo_send, halo_recv, send_a, recv_a, send_b, recv_b, send_z, recv_z, send_g, recv_g,
):
    nx, nz, ny = dims
    place = lax.axis_index("space")
    y, z, x = place % ny, place // ny % nz, place // (ny * nz)
    after, before = (place + 1) % count, (place + count - 1) % count
    ys = [peer(place, dims, "y", d) for d in range(1, ny)]
    xs = [peer(place, dims, "x", d) for d in range(1, nx)]
    zs = [peer(place, dims, "z", d) for d in range(1, nz)]
    greet([after, before] + ys + xs + zs)

    first = []
    for d in range(1, ny):
        first.append(
            push(part_a.at[(y + d) % ny], got_a1.at[d - 1], send_a.at[0, d - 1], recv_a.at[0, d - 1], ys[d - 1])
        )
    for d in range(1, nx):
        first.append(
            push(part_b.at[(x + d) % nx], got_b1.at[d - 1], send_b.at[0, d - 1], recv_b.at[0, d - 1], xs[d - 1])
        )
    halos = [
        push(grad_pre.at[:, pl.ds(HALF, HALF)], prev_p, halo_send.at[0], halo_recv.at[0], after),
        push(grad_pre.at[:, pl.ds(0, HALF)], next_p, halo_send.at[1], halo_recv.at[1], before),
        push(coarse, coarse_in, halo_send.at[2], halo_recv.at[2], before),
    ]
    for copy in first:
        copy.wait()
    size_a, size_b = ROWS_A // (ny * nx), ROWS_B // (ny * nx)
    total = part_a[y]
    for d in range(ny - 1):
        total += got_a1[d]
    for i in range(nx):
        sum_a1[i] = total[i * size_a : (i + 1) * size_a]
    total = part_b[x]
    for d in range(nx - 1):
        total += got_b1[d]
    for i in range(ny):
        sum_b1[i] = total[i * size_b : (i + 1) * size_b]
    second = []
    for d in range(1, nx):
        second.append(
            push(sum_a1.at[(x + d) % nx], got_a2.at[d - 1], send_a.at[1, d - 1], recv_a.at[1, d - 1], xs[d - 1])
        )
    for d in range(1, ny):
        second.append(
            push(sum_b1.at[(y + d) % ny], got_b2.at[d - 1], send_b.at[1, d - 1], recv_b.at[1, d - 1], ys[d - 1])
        )
    for copy in second:
        copy.wait()
    total = sum_a1[x]
    for d in range(nx - 1):
        total += got_a2[d]
    got_z[z, 0:size_a, :] = total
    total = sum_b1[y]
    for d in range(ny - 1):
        total += got_b2[d]
    got_z[z, size_a : size_a + size_b, :] = total

    third = [
        push(got_z.at[z], got_z.at[z], send_z.at[d - 1], recv_z.at[d - 1], zs[d - 1])
        for d in range(1, nz)
    ]
    for copy in third:
        copy.wait()
    total = got_z[0]
    for i in range(1, nz):
        total += got_z[i]
    done[x, y, 0, 0:size_a, :] = total[0:size_a].astype(BF16)
    done[x, y, 1, 0:size_b, :] = total[size_a : size_a + size_b].astype(BF16)

    fourth = [
        push(done.at[x, y, 0], done.at[x, y, 0], send_g.at[0, d - 1], recv_g.at[0, d - 1], xs[d - 1])
        for d in range(1, nx)
    ] + [
        push(done.at[x, y, 1], done.at[x, y, 1], send_g.at[1, d - 1], recv_g.at[1, d - 1], ys[d - 1])
        for d in range(1, ny)
    ]
    for copy in fourth:
        copy.wait()
    fifth = [
        push(done.at[:, y, 0], done.at[:, y, 0], send_g.at[2, d - 1], recv_g.at[2, d - 1], ys[d - 1])
        for d in range(1, ny)
    ] + [
        push(done.at[x, :, 1], done.at[x, :, 1], send_g.at[3, d - 1], recv_g.at[3, d - 1], xs[d - 1])
        for d in range(1, nx)
    ]
    for copy in fifth + halos:
        copy.wait()


def finish_kernel(
    dims, scale, flag, grad_pre, prev_p, next_p, table, prev_t, next_t, nbr, w_conv, back, coarse_own,
    coarse_in, done, coarse_out, grad_feats, grad_conv, grad_down,
    own_hot, prev_hot, next_hot, wide, taps, weights, spill, flat,
):
    nx, _, ny = dims
    cell_maps(table, prev_t, next_t, own_hot, prev_hot, next_hot)
    masks = edge_masks()
    wide[:, 0:LAYER] = dot_nt(prev_p[...], prev_hot[...])
    wide[:, LAYER : LAYER + CELLS] = dot_nt(grad_pre[...], own_hot[...])
    wide[:, LAYER + CELLS : WIDE] = dot_nt(next_p[...], next_hot[...])
    unfold(wide, masks, taps)
    for layer in range(3):
        for tap in range(9):
            k = 26 - (layer * 9 + tap)
            weights[tap * C : (tap + 1) * C, layer * C : (layer + 1) * C] = w_conv[
                :, k * C : (k + 1) * C
            ]
    spill[...] = to_voxels(fold(dot_tn(weights[...], taps[...])), own_hot)

    @pl.when(flag[0] > 0)
    def _():
        rows = jnp.concatenate([prev_p[...], grad_pre[...], next_p[...]], axis=1)
        spill[...] = dot_tn(
            w_conv[:, 26 * C : 27 * C], named_rows(nbr[0:1, :], own_hot, rows)
        )

        def pair(i, carry):
            block = w_conv[:, pl.ds(pl.multiple_of(i * 128, 128), 128)]
            for half in range(2):
                read = named_rows(nbr[pl.ds(26 - 2 * i - half, 1), :], own_hot, rows)
                spill[...] += dot_tn(block[:, half * C : (half + 1) * C], read)
            return carry

        lax.fori_loop(0, 13, pair, 0)

    grad_feats[...] = (back[...] + spill[...]).astype(BF16)
    coarse_out[...] = (coarse_own[...] + coarse_in[...].astype(F32)).astype(BF16)
    size_a, size_b = ROWS_A // (ny * nx), ROWS_B // (ny * nx)
    for i in range(nx):
        for j in range(ny):
            at = (j * nx + i) * size_a
            flat[at : at + size_a, :] = done[i, j, 0, 0:size_a, :].astype(F32) * scale
            at = ROWS_A + (i * ny + j) * size_b
            flat[at : at + size_b, :] = done[i, j, 1, 0:size_b, :].astype(F32) * scale
    for t in range(13):
        grad_conv[:, t * 128 : (t + 1) * 128] = flat[t * C : (t + 1) * C, :]
    grad_conv[:, 13 * 128 : 27 * C] = flat[13 * C : 14 * C, 0:C]
    grad_down[...] = flat[14 * C : 14 * C + 8 * C, :]


def vmem(n):
    return [pl.BlockSpec(memory_space=pltpu.VMEM)] * n


def shape(dims, dtype):
    return jax.ShapeDtypeStruct(dims, dtype)


def per_device(feats, w_conv, w_down, neighbors, parent, octant, grad_out):
    count = lax.axis_size("space")
    dims = CHIPS[count]
    nx, nz, ny = dims
    place = lax.axis_index("space")
    feats, w_conv = feats.T, w_conv.T

    own_start = place * VC
    prev_start = (place - 1) % count * VC
    inside = (parent >= own_start) & (parent < own_start + VC)
    coarse = jnp.where(inside, parent - own_start + VC, parent - prev_start)
    layer = coarse // 128 - 1
    cell = (
        (2 * layer + octant // 4) * LAYER
        + (2 * (coarse % 128 // 8) + octant // 2 % 2) * SZ
        + 2 * (coarse % 8)
        + octant % 2
    )
    cell = jnp.where((layer == 0) | (layer == 1), cell, -1)
    ones = jnp.ones_like(cell)
    zeros = jnp.zeros_like(cell)
    table = jnp.stack(
        [
            cell, coarse, octant,
            jnp.where(place > 0, ones, zeros), jnp.where(place < count - 1, ones, zeros),
            zeros, zeros, zeros,
        ]
    ).astype(F32)

    dma = pltpu.SemaphoreType.DMA
    prev_f, next_f, prev_t, next_t, prev_g = pl.pallas_call(
        functools.partial(halo_kernel, count),
        name="halo",
        out_shape=(
            shape((C, HALF), BF16), shape((C, HALF), BF16),
            shape((8, HALF), F32), shape((8, HALF), F32), shape((VC, C2), BF16),
        ),
        in_specs=vmem(3),
        out_specs=tuple(vmem(5)),
        scratch_shapes=[dma((5,)), dma((5,))],
        compiler_params=pltpu.CompilerParams(collective_id=0, has_side_effects=True),
    )(feats, table, grad_out)

    maps = [
        pltpu.VMEM((CELLS, V), BF16), pltpu.VMEM((LAYER, HALF), BF16), pltpu.VMEM((LAYER, HALF), BF16),
    ]
    grad_pre, back, part_a, part_b, coarse_own, coarse_prev, flag = pl.pallas_call(
        block_kernel,
        name="block",
        out_shape=(
            shape((C, V), BF16), shape((C, V), F32), shape((ROWS_A, C2), F32), shape((ROWS_B, C2), F32),
            shape((VC, C2), F32), shape((VC, C2), BF16), shape((1,), jnp.int32),
        ),
        in_specs=vmem(11),
        out_specs=tuple(vmem(6) + [pl.BlockSpec(memory_space=pltpu.SMEM)]),
        scratch_shapes=maps
        + [
            pltpu.VMEM((C + 8, WIDE), F32), pltpu.VMEM((TAPS, WIDE), BF16), pltpu.VMEM((3 * C, WIDE), BF16),
            pltpu.VMEM((32, V), jnp.int32), pltpu.VMEM((C, V), F32), pltpu.VMEM((C, 28 * C), F32),
            pltpu.VMEM((2 * VC, C2), BF16), pltpu.VMEM((2 * VC, V), BF16), pltpu.VMEM((8 * C, V), BF16),
        ],
    )(feats, prev_f, next_f, table, prev_t, next_t, neighbors, w_conv, w_down, grad_out, prev_g)

    size_a, size_b = ROWS_A // (nx * ny), ROWS_B // (nx * ny)
    most = max(nx, ny) - 1
    prev_p, next_p, coarse_in, done = pl.pallas_call(
        functools.partial(total_kernel, count, dims),
        name="total",
        out_shape=(
            shape((C, HALF), BF16), shape((C, HALF), BF16), shape((VC, C2), BF16),
            shape((nx, ny, 2, size_a, C2), BF16),
        ),
        in_specs=vmem(4),
        out_specs=tuple(vmem(4)),
        scratch_shapes=[
            pltpu.VMEM((ny - 1, ROWS_A // ny, C2), F32), pltpu.VMEM((nx - 1, ROWS_B // nx, C2), F32),
            pltpu.VMEM((nx, size_a, C2), F32), pltpu.VMEM((ny, size_b, C2), F32),
            pltpu.VMEM((nx - 1, size_a, C2), F32), pltpu.VMEM((ny - 1, size_b, C2), F32),
            pltpu.VMEM((nz, size_a + size_b, C2), F32),
            dma((3,)), dma((3,)), dma((2, most)), dma((2, most)), dma((2, most)), dma((2, most)),
            dma((nz - 1,)), dma((nz - 1,)), dma((4, most)), dma((4, most)),
        ],
        compiler_params=pltpu.CompilerParams(collective_id=1, has_side_effects=True),
    )(
        grad_pre, coarse_prev,
        part_a.reshape(ny, ROWS_A // ny, C2), part_b.reshape(nx, ROWS_B // nx, C2),
    )

    coarse_out, grad_feats, grad_conv, grad_down = pl.pallas_call(
        functools.partial(finish_kernel, dims, 1.0 / math.sqrt(V * count)),
        name="finish",
        out_shape=(
            shape((VC, C2), BF16), shape((C, V), BF16), shape((C, 27 * C), F32), shape((8 * C, C2), F32),
        ),
        in_specs=[pl.BlockSpec(memory_space=pltpu.SMEM)] + vmem(12),
        out_specs=tuple(vmem(4)),
        scratch_shapes=maps
        + [
            pltpu.VMEM((C, WIDE), F32), pltpu.VMEM((TAPS, WIDE), BF16), pltpu.VMEM((TAPS, 3 * C), BF16),
            pltpu.VMEM((C, V), F32), pltpu.VMEM((ROWS_A + ROWS_B, C2), F32),
        ],
    )(
        flag, grad_pre, prev_p, next_p, table, prev_t, next_t, neighbors, w_conv, back, coarse_own,
        coarse_in, done,
    )
    return coarse_out, grad_feats.T, grad_conv.T, grad_down


def solution(mesh):
    rows = P(("dp", "space"), None)
    line = P(("dp", "space"))
    return jax.shard_map(
        per_device,
        mesh=mesh,
        in_specs=(rows, P(), P(), P(None, ("dp", "space")), line, line, rows),
        out_specs=(rows, rows, P("dp", None), P("dp", None)),
        check_vma=False,
    )
```

```python
import functools
import math

import jax
import jax.numpy as jnp
from jax import lax
from jax.experimental import pallas as pl
from jax.experimental.pallas import tpu as pltpu
from jax.sharding import PartitionSpec as P

F32 = jnp.float32
BF16 = jnp.bfloat16
C = 64
C2 = 128
V = 1024
HALF = 512
VC = 256
SY, SZ = 32, 16
LAYER = SY * SZ
CELLS = 4 * LAYER
WIDE = CELLS + 2 * LAYER
EMPTY = 3 * V
TAPS = 9 * C
ROWS_A, ROWS_B = 768, 640
CHIPS = {128: (4, 8, 4), 16: (2, 2, 4)}


def dot(a, b):
    return jnp.dot(a, b, preferred_element_type=F32)


def dot_nt(a, b):
    return lax.dot_general(a, b, (((1,), (1,)), ((), ())), preferred_element_type=F32)


def dot_tn(a, b):
    return lax.dot_general(a, b, (((0,), (0,)), ((), ())), preferred_element_type=F32)


def fill_hot(ref, ids, first):
    high = jnp.broadcast_to(
        lax.shift_right_arithmetic(ids, 4).astype(F32).astype(BF16), (16, ids.shape[1])
    )
    row = lax.broadcasted_iota(jnp.int32, high.shape, 0)
    low = jnp.where(row == (ids & 15), 1.0, 0.0).astype(BF16)
    none = jnp.zeros_like(low)
    for t in range(ref.shape[0] // 16):
        ref[t * 16 : (t + 1) * 16, :] = jnp.where(
            high == jnp.asarray(first // 16 + t, BF16), low, none
        )


def peer(place, dims, axis, step):
    _, nz, ny = dims
    y, z, x = place % ny, place // ny % nz, place // (ny * nz)
    if axis == "y":
        return place - y + (y + step) % ny
    if axis == "z":
        return place + ((z + step) % nz - z) * ny
    return place + ((x + step) % dims[0] - x) * (ny * nz)


def greet(partners):
    barrier = pltpu.get_barrier_semaphore()
    for other in partners:
        pl.semaphore_signal(
            barrier, inc=1, device_id={"space": other}, device_id_type=pl.DeviceIdType.MESH
        )
    pl.semaphore_wait(barrier, len(partners))


def push(src, dst, send, recv, other):
    copy = pltpu.make_async_remote_copy(
        src_ref=src,
        dst_ref=dst,
        send_sem=send,
        recv_sem=recv,
        device_id={"space": other},
        device_id_type=pl.DeviceIdType.MESH,
    )
    copy.start()
    return copy


def places(count, place, parent, octant):
    own, prev = place * VC, (place + count - 1) % count * VC
    inside = (parent >= own) & (parent < own + VC)
    coarse = jnp.where(inside, parent - own + VC, parent - prev)
    layer = lax.shift_right_arithmetic(coarse, 7) - 1
    cell = (
        (2 * layer + lax.shift_right_arithmetic(octant, 2)) * LAYER
        + (2 * lax.shift_right_arithmetic(coarse & 127, 3) + (lax.shift_right_arithmetic(octant, 1) & 1)) * SZ
        + 2 * (coarse & 7)
        + (octant & 1)
    )
    return coarse, jnp.where((layer == 0) | (layer == 1), cell, -1)


def edge_masks():
    lane = lax.broadcasted_iota(jnp.int32, (1, LAYER), 1)
    y, z = lax.shift_right_arithmetic(lane, 4), lane & (SZ - 1)
    masks = []
    for dy in (-1, 0, 1):
        for dz in (-1, 0, 1):
            inside = (y + dy >= 0) & (y + dy < SY) & (z + dz >= 0) & (z + dz < SZ)
            masks.append(jnp.where(inside, 1.0, 0.0))
    return masks


def shifted(block, tap, masks):
    step = (tap // 3 - 1) * SZ + tap % 3 - 1
    if step == 0:
        return block
    rows = block.shape[0]
    mask = jnp.broadcast_to(masks[tap], (rows, LAYER)).astype(block.dtype)
    return pltpu.roll(block, (-step) % WIDE, 1) * jnp.concatenate([mask] * (WIDE // LAYER), axis=1)


def unfold(wide, masks, taps):
    for group in range(0, C, 16):
        block = wide[group : group + 16, :]
        for tap in range(9):
            taps[tap * C + group : tap * C + group + 16, :] = shifted(block, tap, masks)


def split(x):
    high = x.astype(BF16)
    return high, (x - high.astype(F32)).astype(BF16)


def named_rows(names, rows, candidates):
    fill_hot(rows, names, HALF)
    return dot(candidates, rows[...]).astype(BF16)


def pieces(ids):
    return lax.shift_right_logical(ids, 6).astype(F32), (ids & 63).astype(F32)


def octant_order(flip):
    shape_ = (256, 256)
    cell = lax.broadcasted_iota(jnp.int32, shape_, 1 if flip else 0)
    slot = lax.broadcasted_iota(jnp.int32, shape_, 0 if flip else 1)
    corner, pair = lax.shift_right_arithmetic(slot, 6), slot & 63
    y = 2 * lax.shift_right_arithmetic(pair, 3) + lax.shift_right_arithmetic(corner, 1)
    z = 2 * (pair & 7) + (corner & 1)
    return jnp.where(cell == y * SZ + z, 1.0, 0.0).astype(BF16)


def store_conv(conv, part_a, part_b):
    for t in range(12):
        part_a[t * C : (t + 1) * C, :] = conv[:, t * 128 : (t + 1) * 128]
    for t in range(2):
        part_b[t * C : (t + 1) * C, :] = conv[:, (12 + t) * 128 : (13 + t) * 128]


def block_kernel(
    count, feats, parent, octant, nbr, w_conv, w_down, grads,
    grad_pre, slopes, back, part_a, part_b, coarse_own, coarse_prev, wrong, table, edges,
    prev_f, next_f, prev_g,
    prev_p, next_p, prev_o, next_o, own_hot, prev_hot, next_hot, wide, ids, seen, taps, stack, named,
    conv, spread, lookup, send, recv,
):
    place = lax.axis_index("space")
    after, before = (place + 1) % count, (place + count - 1) % count
    greet((after, before))
    late, early = pl.ds(HALF, HALF), pl.ds(0, HALF)
    marks = [
        push(parent.at[:, late], prev_p, send.at[0], recv.at[0], after),
        push(octant.at[:, late], prev_o, send.at[1], recv.at[1], after),
        push(parent.at[:, early], next_p, send.at[2], recv.at[2], before),
        push(octant.at[:, early], next_o, send.at[3], recv.at[3], before),
    ]
    halos = [
        push(feats.at[:, late], prev_f, send.at[4], recv.at[4], after),
        push(feats.at[:, early], next_f, send.at[5], recv.at[5], before),
    ]
    coarse_halo = push(grads, prev_g, send.at[6], recv.at[6], after)

    coarse, cell = places(count, place, parent[...], octant[...])
    table[...] = jnp.zeros_like(table)
    table[0:1, :] = cell.astype(F32)
    table[1:2, :] = coarse.astype(F32)
    table[2:3, :] = octant[...].astype(F32)
    fill_hot(own_hot, cell, 0)
    masks = edge_masks()
    lane = lax.broadcasted_iota(jnp.int32, (1, V), 1)
    named[...] = jnp.zeros_like(named)
    named[0:27, :] = EMPTY - nbr[...]
    named[27:28, :] = 2 * V - lane
    high, low = pieces(named[...])
    own = jnp.concatenate([feats[...], high.astype(BF16), low.astype(BF16)], axis=0)
    own = dot_nt(own, own_hot[...])
    wide[:, LAYER : LAYER + CELLS] = own[0:C].astype(BF16)
    told = own[C : C + 32] * 64.0 + own[C + 32 : C + 64]
    occupied = told[27:28] > 0.0
    ids[:, LAYER : LAYER + CELLS] = jnp.broadcast_to(told[27:28], (8, CELLS))

    for copy in marks:
        copy.wait()
    _, prev_cell = places(count, before, prev_p[...], prev_o[...])
    _, next_cell = places(count, after, next_p[...], next_o[...])
    prev_cell = jnp.where(place > 0, prev_cell, -1)
    next_cell = jnp.where(place < count - 1, next_cell, -1)
    edges[...] = jnp.zeros_like(edges)
    edges[0:1, 0:HALF] = prev_cell.astype(F32)
    edges[0:1, HALF:V] = next_cell.astype(F32)
    fill_hot(prev_hot, prev_cell, 3 * LAYER)
    fill_hot(next_hot, next_cell, 0)
    for copy in halos:
        copy.wait()
    row = lax.broadcasted_iota(jnp.int32, (16, HALF), 0)
    half_lane = lax.broadcasted_iota(jnp.int32, (16, HALF), 1)
    for edge, where_hot, names, at in (
        (prev_f, prev_hot, EMPTY - HALF - half_lane, 0),
        (next_f, next_hot, V - half_lane, LAYER + CELLS),
    ):
        high, low = pieces(names)
        tail = jnp.where(row == 0, high, jnp.where(row == 1, low, 0.0)).astype(BF16)
        placed = dot_nt(jnp.concatenate([edge[...], tail], axis=0), where_hot[...])
        wide[:, at : at + LAYER] = placed[0:C].astype(BF16)
        ids[:, at : at + LAYER] = jnp.broadcast_to(
            placed[C : C + 1] * 64.0 + placed[C + 1 : C + 2], (8, LAYER)
        )

    for tap in range(9):
        seen[tap * 8 : (tap + 1) * 8, :] = shifted(ids[...], tap, masks)
    row = lax.broadcasted_iota(jnp.int32, (8, CELLS), 0)
    worst = jnp.zeros((8, CELLS), F32)
    for group in range(4):
        expect = jnp.zeros((8, CELLS), F32)
        for k in range(group * 8, min(group * 8 + 8, 27)):
            layer, tap = k // 9, k % 9
            expect = jnp.where(
                row == k % 8, seen[tap * 8 : (tap + 1) * 8, layer * LAYER : layer * LAYER + CELLS], expect
            )
        differs = jnp.abs(told[group * 8 : group * 8 + 8] - expect)
        if group == 3:
            differs = jnp.where(row < 3, differs, 0.0)
        worst = jnp.maximum(worst, differs)
    worst = jnp.where(jnp.broadcast_to(occupied, (8, CELLS)), worst, 0.0)
    wrong[0] = jnp.maximum(jnp.max(worst), jnp.max(-cell.astype(F32)))

    unfold(wide, masks, taps)
    weights = jnp.concatenate([w_conv[:, d * TAPS : (d + 1) * TAPS] for d in range(3)], axis=0)
    spread[...] = dot(weights, taps[...])

    coarse_halo.wait()
    lookup[0:128, :] = prev_g[128:VC, :]
    lookup[128:VC, :] = grads[0:128, :]
    product = dot_nt(w_down[...], lookup[...])
    blocks = []
    for b in range(8):
        h, at = b // 2 % 2, b // 4 * 128 + b % 2 * C
        blocks.append(
            jnp.concatenate(
                [product[(h * 4 + q) * C : (h * 4 + q + 1) * C, at : at + C] for q in range(4)], axis=1
            )
        )
    high, low = split(jnp.concatenate(blocks, axis=0))
    spread_back = octant_order(True)
    rows = dot(high, spread_back) + dot(low, spread_back)
    for b in range(8):
        back[:, b * 256 : (b + 1) * 256] = rows[b * C : (b + 1) * C]

    middles = []
    for b in range(8):
        at = b * 256
        act = (
            spread[0:C, at : at + 256]
            + spread[C : 2 * C, LAYER + at : LAYER + at + 256]
            + spread[2 * C : 3 * C, 2 * LAYER + at : 2 * LAYER + at + 256]
        )
        here = jnp.broadcast_to(occupied[:, at : at + 256], (C, 256))
        gate = jax.nn.sigmoid(act)
        held = wide[:, LAYER + at : LAYER + at + 256].astype(F32)
        middles.append(jnp.where(here, held + act * gate, 0.0).astype(BF16))
        slope = back[:, at : at + 256] * gate * (1.0 + act * (1.0 - gate))
        slopes[:, at : at + 256] = jnp.where(here, slope, 0.0).astype(BF16)

    sorted_ = dot(jnp.concatenate(middles, axis=0), octant_order(False)).astype(BF16)
    children = jnp.concatenate(
        [
            jnp.concatenate(
                [
                    sorted_[b * C : (b + 1) * C, q * C : (q + 1) * C]
                    for b in (2 * h, 2 * h + 1, 4 + 2 * h, 5 + 2 * h)
                ],
                axis=1,
            )
            for h in range(2)
            for q in range(4)
        ],
        axis=0,
    )
    sums = dot_tn(children, w_down[...])
    coarse_prev[0:128, :] = jnp.zeros((128, C2), BF16)
    coarse_prev[128:VC, :] = sums[0:128].astype(BF16)
    coarse_own[0:128, :] = sums[128:VC]
    coarse_own[128:VC, :] = jnp.zeros((128, C2), F32)
    part_b[128:ROWS_B, :] = dot(children, lookup[...])

    turned = slopes[...].T
    stack[...] = jnp.zeros_like(stack)
    for d in range(3):
        stack[d * LAYER : d * LAYER + CELLS, d * C : (d + 1) * C] = turned
    product = dot(taps[...], stack[...])
    conv[:, 27 * C : 28 * C] = jnp.zeros((C, C), F32)
    conv[:, 0 : 27 * C] = jnp.concatenate([product[:, d * C : (d + 1) * C].T for d in range(3)], axis=1)
    store_conv(conv, part_a, part_b)
    grad_pre[...] = dot(slopes[...], own_hot[...]).astype(BF16)


def repair_kernel(
    wrong, feats, prev_f, next_f, table, nbr, w_conv, w_down, grads, prev_g,
    old_pre, old_a, old_b, old_own, old_prev,
    grad_pre, part_a, part_b, coarse_own, coarse_prev, back,
    feats_v, cand, table_v, nbr_v, conv_v, down_v, lookup, rows, preact, slope_v, back_v, conv, spread, parent_hot,
    part_a_v, part_b_v, own_v, prev_v,
):
    @pl.when(wrong[0] > 0.0)
    def _():
        for src, dst in (
            (feats, feats_v), (prev_f, cand.at[:, pl.ds(0, HALF)]), (feats, cand.at[:, pl.ds(HALF, V)]),
            (next_f, cand.at[:, pl.ds(HALF + V, HALF)]), (table, table_v), (nbr, nbr_v), (w_conv, conv_v),
            (w_down, down_v), (prev_g, lookup.at[pl.ds(0, VC)]), (grads, lookup.at[pl.ds(VC, VC)]),
        ):
            pltpu.sync_copy(src, dst)
        preact[...] = dot(conv_v[:, 26 * C : 27 * C], named_rows(nbr_v[26:27, :], rows, cand[...]))

        def forward(i, carry):
            block = conv_v[:, pl.ds(pl.multiple_of(i * 128, 128), 128)]
            for half in range(2):
                read = named_rows(nbr_v[pl.ds(2 * i + half, 1), :], rows, cand[...])
                preact[...] += dot(block[:, half * C : (half + 1) * C], read)
            return carry

        lax.fori_loop(0, 13, forward, 0)
        act = preact[...]
        gate = jax.nn.sigmoid(act)
        middle = feats_v[...].astype(F32) + act * gate
        fill_hot(parent_hot, table_v[1:2, :].astype(jnp.int32), 0)
        parent_grads = dot_tn(lookup[...], parent_hot[...]).astype(BF16)
        back_all = dot(down_v[...], parent_grads)
        octant = table_v[2:3, :]
        total = jnp.zeros((C, V), F32)
        for o in range(8):
            chosen = jnp.broadcast_to(octant == float(o), (C, V))
            total += jnp.where(chosen, back_all[o * C : (o + 1) * C], 0.0)
            spread[o * C : (o + 1) * C, :] = jnp.where(chosen, middle, 0.0).astype(BF16)
        back_v[...] = total
        children = dot_nt(spread[...], parent_hot[...]).astype(BF16)
        sums = dot_tn(children, down_v[...])
        prev_v[...] = sums[0:VC].astype(BF16)
        own_v[...] = sums[VC : 2 * VC]
        part_b_v[128:ROWS_B, :] = dot(children, lookup[...])
        slope_v[...] = (total * gate * (1.0 + act * (1.0 - gate))).astype(BF16)

        def weight(i, carry):
            both = [
                dot_nt(slope_v[...], named_rows(nbr_v[pl.ds(2 * i + half, 1), :], rows, cand[...]))
                for half in range(2)
            ]
            conv[:, pl.ds(pl.multiple_of(i * 128, 128), 128)] = jnp.concatenate(both, axis=1)
            return carry

        lax.fori_loop(0, 13, weight, 0)
        last = dot_nt(slope_v[...], named_rows(nbr_v[26:27, :], rows, cand[...]))
        conv[:, 26 * C : 28 * C] = jnp.concatenate([last, jnp.zeros_like(last)], axis=1)
        store_conv(conv, part_a_v, part_b_v)
        for src, dst in (
            (slope_v, grad_pre), (part_a_v, part_a), (part_b_v, part_b), (own_v, coarse_own),
            (prev_v, coarse_prev), (back_v, back),
        ):
            pltpu.sync_copy(src, dst)


def total_kernel(
    count, dims, grad_pre, slopes, back, coarse_own, coarse, table, edges, w_conv, part_a, part_b,
    prev_p, next_p, coarse_out, grad_feats, done,
    got_a1, got_b1, sum_a1, sum_b1, got_a2, got_b2, got_z, coarse_in,
    own_hot, prev_hot, next_hot, wide, taps, weights, spread,
    halo_send, halo_recv, send_a, recv_a, send_b, recv_b, send_z, recv_z, send_g, recv_g,
):
    nx, nz, ny = dims
    place = lax.axis_index("space")
    y, z, x = place % ny, place // ny % nz, place // (ny * nz)
    after, before = (place + 1) % count, (place + count - 1) % count
    ys = [peer(place, dims, "y", d) for d in range(1, ny)]
    xs = [peer(place, dims, "x", d) for d in range(1, nx)]
    zs = [peer(place, dims, "z", d) for d in range(1, nz)]
    greet([after, before] + ys + xs + zs)

    first = []
    for d in range(1, ny):
        first.append(
            push(part_a.at[(y + d) % ny], got_a1.at[d - 1], send_a.at[0, d - 1], recv_a.at[0, d - 1], ys[d - 1])
        )
    for d in range(1, nx):
        first.append(
            push(part_b.at[(x + d) % nx], got_b1.at[d - 1], send_b.at[0, d - 1], recv_b.at[0, d - 1], xs[d - 1])
        )
    halos = [
        push(grad_pre.at[:, pl.ds(HALF, HALF)], prev_p, halo_send.at[0], halo_recv.at[0], after),
        push(grad_pre.at[:, pl.ds(0, HALF)], next_p, halo_send.at[1], halo_recv.at[1], before),
        push(coarse, coarse_in, halo_send.at[2], halo_recv.at[2], before),
    ]

    fill_hot(own_hot, table[0:1, :].astype(jnp.int32), 0)
    fill_hot(prev_hot, edges[0:1, 0:HALF].astype(jnp.int32), 3 * LAYER)
    fill_hot(next_hot, edges[0:1, HALF:V].astype(jnp.int32), 0)
    for layer in range(3):
        for tap in range(9):
            k = 26 - (layer * 9 + tap)
            weights[tap * C : (tap + 1) * C, layer * C : (layer + 1) * C] = w_conv[:, k * C : (k + 1) * C]

    for copy in first:
        copy.wait()
    size_a, size_b = ROWS_A // (ny * nx), ROWS_B // (ny * nx)
    total = part_a[y]
    for d in range(ny - 1):
        total += got_a1[d]
    for i in range(nx):
        sum_a1[i] = total[i * size_a : (i + 1) * size_a]
    total = part_b[x]
    for d in range(nx - 1):
        total += got_b1[d]
    for i in range(ny):
        sum_b1[i] = total[i * size_b : (i + 1) * size_b]
    second = []
    for d in range(1, nx):
        second.append(
            push(sum_a1.at[(x + d) % nx], got_a2.at[d - 1], send_a.at[1, d - 1], recv_a.at[1, d - 1], xs[d - 1])
        )
    for d in range(1, ny):
        second.append(
            push(sum_b1.at[(y + d) % ny], got_b2.at[d - 1], send_b.at[1, d - 1], recv_b.at[1, d - 1], ys[d - 1])
        )

    for copy in halos:
        copy.wait()
    coarse_out[...] = (coarse_own[...] + coarse_in[...].astype(F32)).astype(BF16)
    wide[:, 0:LAYER] = dot_nt(prev_p[...], prev_hot[...]).astype(BF16)
    wide[:, LAYER : LAYER + CELLS] = slopes[...]
    wide[:, LAYER + CELLS : WIDE] = dot_nt(next_p[...], next_hot[...]).astype(BF16)
    unfold(wide, edge_masks(), taps)

    for copy in second:
        copy.wait()
    total = sum_a1[x]
    for d in range(nx - 1):
        total += got_a2[d]
    got_z[z, 0:size_a, :] = total
    total = sum_b1[y]
    for d in range(ny - 1):
        total += got_b2[d]
    got_z[z, size_a : size_a + size_b, :] = total

    third = [
        push(got_z.at[z], got_z.at[z], send_z.at[d - 1], recv_z.at[d - 1], zs[d - 1])
        for d in range(1, nz)
    ]

    spread[...] = dot_tn(weights[...], taps[...])
    cells = (
        spread[0:C, 0:CELLS]
        + spread[C : 2 * C, LAYER : LAYER + CELLS]
        + spread[2 * C : 3 * C, 2 * LAYER : 2 * LAYER + CELLS]
        + back[...]
    )
    both = dot(jnp.concatenate(split(cells), axis=0), own_hot[...])
    grad_feats[...] = (both[0:C] + both[C : 2 * C]).astype(BF16)

    for copy in third:
        copy.wait()
    total = got_z[0]
    for i in range(1, nz):
        total += got_z[i]
    done[x, y, 0, 0:size_a, :] = total[0:size_a].astype(BF16)
    done[x, y, 1, 0:size_b, :] = total[size_a : size_a + size_b].astype(BF16)

    fourth = [
        push(done.at[x, y, 0], done.at[x, y, 0], send_g.at[0, d - 1], recv_g.at[0, d - 1], xs[d - 1])
        for d in range(1, nx)
    ] + [
        push(done.at[x, y, 1], done.at[x, y, 1], send_g.at[1, d - 1], recv_g.at[1, d - 1], ys[d - 1])
        for d in range(1, ny)
    ]
    for copy in fourth:
        copy.wait()
    fifth = [
        push(done.at[:, y, 0], done.at[:, y, 0], send_g.at[2, d - 1], recv_g.at[2, d - 1], ys[d - 1])
        for d in range(1, ny)
    ] + [
        push(done.at[x, :, 1], done.at[x, :, 1], send_g.at[3, d - 1], recv_g.at[3, d - 1], xs[d - 1])
        for d in range(1, nx)
    ]
    for copy in fifth:
        copy.wait()


def finish_kernel(
    dims, scale, wrong, grad_fast, coarse, done, grad_pre, prev_p, next_p, nbr, w_conv, back,
    coarse_out, grad_feats, grad_conv, grad_down,
    flat, cand, nbr_v, conv_v, spill, rows,
):
    nx, _, ny = dims
    coarse_out[...] = coarse[...]
    grad_feats[...] = grad_fast[...]
    size_a, size_b = ROWS_A // (ny * nx), ROWS_B // (ny * nx)
    for i in range(nx):
        for j in range(ny):
            at = (j * nx + i) * size_a
            flat[at : at + size_a, :] = done[i, j, 0, 0:size_a, :].astype(F32) * scale
            at = ROWS_A + (i * ny + j) * size_b
            flat[at : at + size_b, :] = done[i, j, 1, 0:size_b, :].astype(F32) * scale
    for t in range(13):
        grad_conv[:, t * 128 : (t + 1) * 128] = flat[t * C : (t + 1) * C, :]
    grad_conv[:, 13 * 128 : 27 * C] = flat[13 * C : 14 * C, 0:C]
    grad_down[...] = flat[14 * C : 14 * C + 8 * C, :]

    @pl.when(wrong[0] > 0.0)
    def _():
        for src, dst in (
            (prev_p, cand.at[:, pl.ds(0, HALF)]), (grad_pre, cand.at[:, pl.ds(HALF, V)]),
            (next_p, cand.at[:, pl.ds(HALF + V, HALF)]), (nbr, nbr_v), (w_conv, conv_v), (back, spill),
        ):
            pltpu.sync_copy(src, dst)
        spill[...] += dot_tn(conv_v[:, 26 * C : 27 * C], named_rows(nbr_v[0:1, :], rows, cand[...]))

        def pull(i, carry):
            block = conv_v[:, pl.ds(pl.multiple_of(i * 128, 128), 128)]
            for half in range(2):
                read = named_rows(nbr_v[pl.ds(26 - 2 * i - half, 1), :], rows, cand[...])
                spill[...] += dot_tn(block[:, half * C : (half + 1) * C], read)
            return carry

        lax.fori_loop(0, 13, pull, 0)
        grad_feats[...] = spill[...].astype(BF16)


def vmem(n):
    return [pl.BlockSpec(memory_space=pltpu.VMEM)] * n


def anywhere(n):
    return [pl.BlockSpec(memory_space=pl.ANY)] * n


def shape(dims, dtype):
    return jax.ShapeDtypeStruct(dims, dtype)


GRANT = 32 * 1024 * 1024


def per_device(feats, w_conv, w_down, neighbors, parent, octant, grad_out):
    count = lax.axis_size("space")
    dims = CHIPS[count]
    nx, nz, ny = dims
    feats, w_conv = feats.T, w_conv.T
    parent, octant = parent.reshape(1, V), octant.reshape(1, V)
    dma = pltpu.SemaphoreType.DMA
    smem = [pl.BlockSpec(memory_space=pltpu.SMEM)]
    maps = [
        pltpu.VMEM((CELLS, V), BF16), pltpu.VMEM((LAYER, HALF), BF16), pltpu.VMEM((LAYER, HALF), BF16),
    ]
    half, row_half = shape((C, HALF), BF16), pltpu.VMEM((1, HALF), jnp.int32)

    (
        grad_pre, slopes, back, part_a, part_b, coarse_own, coarse_prev, wrong, table, edges,
        prev_f, next_f, prev_g,
    ) = pl.pallas_call(
        functools.partial(block_kernel, count),
        name="block",
        out_shape=(
            shape((C, V), BF16), shape((C, CELLS), BF16), shape((C, CELLS), F32),
            shape((ROWS_A, C2), F32), shape((ROWS_B, C2), F32), shape((VC, C2), F32), shape((VC, C2), BF16),
            shape((1,), F32), shape((8, V), F32), shape((8, V), F32), half, half, shape((VC, C2), BF16),
        ),
        in_specs=vmem(7),
        out_specs=tuple(vmem(7) + smem + vmem(5)),
        scratch_shapes=[row_half] * 4
        + maps
        + [
            pltpu.VMEM((C, WIDE), BF16), pltpu.VMEM((8, WIDE), F32), pltpu.VMEM((72, WIDE), F32),
            pltpu.VMEM((TAPS, WIDE), BF16), pltpu.VMEM((WIDE, 3 * C), BF16), pltpu.VMEM((32, V), jnp.int32),
            pltpu.VMEM((C, 28 * C), F32), pltpu.VMEM((3 * C, WIDE), F32), pltpu.VMEM((VC, C2), BF16),
            dma((7,)), dma((7,)),
        ],
        compiler_params=pltpu.CompilerParams(
            collective_id=0, has_side_effects=True, vmem_limit_bytes=GRANT
        ),
    )(feats, parent, octant, neighbors, w_conv, w_down, grad_out)

    grad_pre, part_a, part_b, coarse_own, coarse_prev, back_general = pl.pallas_call(
        repair_kernel,
        name="repair",
        out_shape=(
            shape((C, V), BF16), shape((ROWS_A, C2), F32), shape((ROWS_B, C2), F32),
            shape((VC, C2), F32), shape((VC, C2), BF16), shape((C, V), F32),
        ),
        in_specs=smem + anywhere(14),
        out_specs=tuple(anywhere(6)),
        input_output_aliases={10: 0, 11: 1, 12: 2, 13: 3, 14: 4},
        scratch_shapes=[
            pltpu.VMEM((C, V), BF16), pltpu.VMEM((C, 2 * V), BF16), pltpu.VMEM((8, V), F32),
            pltpu.VMEM((27, V), jnp.int32), pltpu.VMEM((C, 27 * C), BF16), pltpu.VMEM((8 * C, C2), BF16),
            pltpu.VMEM((2 * VC, C2), BF16), pltpu.VMEM((CELLS, V), BF16), pltpu.VMEM((C, V), F32),
            pltpu.VMEM((C, V), BF16), pltpu.VMEM((C, V), F32), pltpu.VMEM((C, 28 * C), F32),
            pltpu.VMEM((8 * C, V), BF16), pltpu.VMEM((2 * VC, V), BF16),
            pltpu.VMEM((ROWS_A, C2), F32), pltpu.VMEM((ROWS_B, C2), F32), pltpu.VMEM((VC, C2), F32),
            pltpu.VMEM((VC, C2), BF16),
        ],
        compiler_params=pltpu.CompilerParams(vmem_limit_bytes=GRANT),
    )(
        wrong, feats, prev_f, next_f, table, neighbors, w_conv, w_down, grad_out, prev_g,
        grad_pre, part_a, part_b, coarse_own, coarse_prev,
    )

    size_a, size_b = ROWS_A // (nx * ny), ROWS_B // (nx * ny)
    most = max(nx, ny) - 1
    prev_p, next_p, coarse_out, grad_feats, done = pl.pallas_call(
        functools.partial(total_kernel, count, dims),
        name="total",
        out_shape=(
            half, half, shape((VC, C2), BF16), shape((C, V), BF16), shape((nx, ny, 2, size_a, C2), BF16),
        ),
        in_specs=vmem(10),
        out_specs=tuple(vmem(5)),
        scratch_shapes=[
            pltpu.VMEM((ny - 1, ROWS_A // ny, C2), F32), pltpu.VMEM((nx - 1, ROWS_B // nx, C2), F32),
            pltpu.VMEM((nx, size_a, C2), F32), pltpu.VMEM((ny, size_b, C2), F32),
            pltpu.VMEM((nx - 1, size_a, C2), F32), pltpu.VMEM((ny - 1, size_b, C2), F32),
            pltpu.VMEM((nz, size_a + size_b, C2), F32), pltpu.VMEM((VC, C2), BF16),
        ]
        + maps
        + [
            pltpu.VMEM((C, WIDE), BF16), pltpu.VMEM((TAPS, WIDE), BF16), pltpu.VMEM((TAPS, 3 * C), BF16),
            pltpu.VMEM((3 * C, WIDE), F32),
            dma((3,)), dma((3,)), dma((2, most)), dma((2, most)), dma((2, most)), dma((2, most)),
            dma((nz - 1,)), dma((nz - 1,)), dma((4, most)), dma((4, most)),
        ],
        compiler_params=pltpu.CompilerParams(
            collective_id=1, has_side_effects=True, vmem_limit_bytes=GRANT
        ),
    )(
        grad_pre, slopes, back, coarse_own, coarse_prev, table, edges, w_conv,
        part_a.reshape(ny, ROWS_A // ny, C2), part_b.reshape(nx, ROWS_B // nx, C2),
    )

    coarse_out, grad_feats, grad_conv, grad_down = pl.pallas_call(
        functools.partial(finish_kernel, dims, 1.0 / math.sqrt(V * count)),
        name="finish",
        out_shape=(
            shape((VC, C2), BF16), shape((C, V), BF16), shape((C, 27 * C), F32), shape((8 * C, C2), F32),
        ),
        in_specs=smem + vmem(3) + anywhere(6),
        out_specs=tuple(vmem(4)),
        scratch_shapes=[
            pltpu.VMEM((ROWS_A + ROWS_B, C2), F32), pltpu.VMEM((C, 2 * V), BF16),
            pltpu.VMEM((27, V), jnp.int32), pltpu.VMEM((C, 27 * C), BF16), pltpu.VMEM((C, V), F32),
            pltpu.VMEM((CELLS, V), BF16),
        ],
        compiler_params=pltpu.CompilerParams(vmem_limit_bytes=GRANT),
    )(
        wrong, grad_feats, coarse_out, done, grad_pre, prev_p, next_p, neighbors, w_conv, back_general,
    )
    return coarse_out, grad_feats.T, grad_conv.T, grad_down


def solution(mesh):
    rows = P(("dp", "space"), None)
    line = P(("dp", "space"))
    return jax.shard_map(
        per_device,
        mesh=mesh,
        in_specs=(rows, P(), P(), P(None, ("dp", "space")), line, line, rows),
        out_specs=(rows, rows, P("dp", None), P("dp", None)),
        check_vma=False,
    )
```

```python
import functools
import math

import jax
import jax.numpy as jnp
from jax import lax
from jax.experimental import pallas as pl
from jax.experimental.pallas import tpu as pltpu
from jax.sharding import PartitionSpec as P

F32 = jnp.float32
BF16 = jnp.bfloat16
C = 64
C2 = 128
V = 1024
HALF = 512
VC = 256
SY, SZ = 32, 16
LAYER = SY * SZ
CELLS = 4 * LAYER
WIDE = CELLS + 2 * LAYER
EMPTY = 3 * V
TAPS = 9 * C
ROWS_A, ROWS_B = 768, 640
CHIPS = {128: (4, 8, 4), 16: (2, 2, 4)}


def dot(a, b):
    return jnp.dot(a, b, preferred_element_type=F32)


def dot_nt(a, b):
    return lax.dot_general(a, b, (((1,), (1,)), ((), ())), preferred_element_type=F32)


def dot_tn(a, b):
    return lax.dot_general(a, b, (((0,), (0,)), ((), ())), preferred_element_type=F32)


def fill_hot(ref, ids, first):
    high = jnp.broadcast_to(
        lax.shift_right_arithmetic(ids, 4).astype(F32).astype(BF16), (16, ids.shape[1])
    )
    row = lax.broadcasted_iota(jnp.int32, high.shape, 0)
    low = jnp.where(row == (ids & 15), 1.0, 0.0).astype(BF16)
    none = jnp.zeros_like(low)
    for t in range(ref.shape[0] // 16):
        ref[t * 16 : (t + 1) * 16, :] = jnp.where(
            high == jnp.asarray(first // 16 + t, BF16), low, none
        )


def peer(place, dims, axis, step):
    _, nz, ny = dims
    y, z, x = place % ny, place // ny % nz, place // (ny * nz)
    if axis == "y":
        return place - y + (y + step) % ny
    if axis == "z":
        return place + ((z + step) % nz - z) * ny
    return place + ((x + step) % dims[0] - x) * (ny * nz)


def signal(partners):
    barrier = pltpu.get_barrier_semaphore()
    for other in partners:
        pl.semaphore_signal(
            barrier, inc=1, device_id={"space": other}, device_id_type=pl.DeviceIdType.MESH
        )


def await_partners(partners):
    pl.semaphore_wait(pltpu.get_barrier_semaphore(), len(partners))


def push(src, dst, send, recv, other):
    copy = pltpu.make_async_remote_copy(
        src_ref=src,
        dst_ref=dst,
        send_sem=send,
        recv_sem=recv,
        device_id={"space": other},
        device_id_type=pl.DeviceIdType.MESH,
    )
    copy.start()
    return copy


def places(count, place, parent, octant):
    own, prev = place * VC, (place + count - 1) % count * VC
    inside = (parent >= own) & (parent < own + VC)
    coarse = jnp.where(inside, parent - own + VC, parent - prev)
    layer = lax.shift_right_arithmetic(coarse, 7) - 1
    cell = (
        (2 * layer + lax.shift_right_arithmetic(octant, 2)) * LAYER
        + (2 * lax.shift_right_arithmetic(coarse & 127, 3) + (lax.shift_right_arithmetic(octant, 1) & 1)) * SZ
        + 2 * (coarse & 7)
        + (octant & 1)
    )
    return coarse, jnp.where((layer == 0) | (layer == 1), cell, -1)


def edge_masks():
    lane = lax.broadcasted_iota(jnp.int32, (1, LAYER), 1)
    y, z = lax.shift_right_arithmetic(lane, 4), lane & (SZ - 1)
    masks = []
    for dy in (-1, 0, 1):
        for dz in (-1, 0, 1):
            inside = (y + dy >= 0) & (y + dy < SY) & (z + dz >= 0) & (z + dz < SZ)
            masks.append(jnp.where(inside, 1.0, 0.0))
    return masks


def shifted(block, tap, masks):
    step = (tap // 3 - 1) * SZ + tap % 3 - 1
    if step == 0:
        return block
    rows = block.shape[0]
    mask = jnp.broadcast_to(masks[tap], (rows, LAYER)).astype(block.dtype)
    return pltpu.roll(block, (-step) % WIDE, 1) * jnp.concatenate([mask] * (WIDE // LAYER), axis=1)


def unfold(wide, masks, taps):
    for group in range(0, C, 16):
        block = wide[group : group + 16, :]
        for tap in range(9):
            taps[tap * C + group : tap * C + group + 16, :] = shifted(block, tap, masks)


def split(x):
    high = x.astype(BF16)
    return high, (x - high.astype(F32)).astype(BF16)


def named_rows(names, rows, candidates):
    fill_hot(rows, names, HALF)
    return dot(candidates, rows[...]).astype(BF16)


def pieces(ids):
    return lax.shift_right_logical(ids, 6).astype(F32), (ids & 63).astype(F32)


def octant_order(flip):
    shape_ = (256, 256)
    cell = lax.broadcasted_iota(jnp.int32, shape_, 1 if flip else 0)
    slot = lax.broadcasted_iota(jnp.int32, shape_, 0 if flip else 1)
    corner, pair = lax.shift_right_arithmetic(slot, 6), slot & 63
    y = 2 * lax.shift_right_arithmetic(pair, 3) + lax.shift_right_arithmetic(corner, 1)
    z = 2 * (pair & 7) + (corner & 1)
    return jnp.where(cell == y * SZ + z, 1.0, 0.0).astype(BF16)


def store_conv(conv, part_a, part_b):
    for t in range(12):
        part_a[t * C : (t + 1) * C, :] = conv[:, t * 128 : (t + 1) * 128]
    for t in range(2):
        part_b[t * C : (t + 1) * C, :] = conv[:, (12 + t) * 128 : (13 + t) * 128]


def block_kernel(
    count, feats_in, parent_in, octant_in, nbr_in, w_conv_in, w_down_in, grads_in,
    grad_pre, slopes, back, part_a, part_b, coarse_own, coarse_prev, wrong, table, edges,
    prev_f, next_f, prev_g,
    prev_p, next_p, prev_o, next_o, own_hot, prev_hot, next_hot, wide, ids, seen, taps, stack, named,
    conv, spread, lookup, feats, parent, octant, nbr, w_conv, w_down, grads, send, recv, load,
):
    place = lax.axis_index("space")
    after, before = (place + 1) % count, (place + count - 1) % count
    signal((after, before))
    inputs = (
        (parent_in, parent), (octant_in, octant), (feats_in, feats), (grads_in, grads), (nbr_in, nbr),
        (w_conv_in, w_conv), (w_down_in, w_down),
    )
    loads = [pltpu.make_async_copy(src, dst, load.at[i]) for i, (src, dst) in enumerate(inputs)]
    for copy in loads:
        copy.start()
    for copy in loads[0:4]:
        copy.wait()
    await_partners((after, before))
    late, early = pl.ds(HALF, HALF), pl.ds(0, HALF)
    marks = [
        push(parent.at[:, late], prev_p, send.at[0], recv.at[0], after),
        push(octant.at[:, late], prev_o, send.at[1], recv.at[1], after),
        push(parent.at[:, early], next_p, send.at[2], recv.at[2], before),
        push(octant.at[:, early], next_o, send.at[3], recv.at[3], before),
    ]
    halos = [
        push(feats.at[:, late], prev_f, send.at[4], recv.at[4], after),
        push(feats.at[:, early], next_f, send.at[5], recv.at[5], before),
    ]
    coarse_halo = push(grads, prev_g, send.at[6], recv.at[6], after)

    for copy in loads[4:]:
        copy.wait()
    coarse, cell = places(count, place, parent[...], octant[...])
    table[...] = jnp.zeros_like(table)
    table[0:1, :] = cell.astype(F32)
    table[1:2, :] = coarse.astype(F32)
    table[2:3, :] = octant[...].astype(F32)
    fill_hot(own_hot, cell, 0)
    masks = edge_masks()
    lane = lax.broadcasted_iota(jnp.int32, (1, V), 1)
    named[...] = jnp.zeros_like(named)
    named[0:27, :] = EMPTY - nbr[...]
    named[27:28, :] = 2 * V - lane
    high, low = pieces(named[...])
    own = jnp.concatenate([feats[...], high.astype(BF16), low.astype(BF16)], axis=0)
    own = dot_nt(own, own_hot[...])
    wide[:, LAYER : LAYER + CELLS] = own[0:C].astype(BF16)
    told = own[C : C + 32] * 64.0 + own[C + 32 : C + 64]
    occupied = told[27:28] > 0.0
    ids[:, LAYER : LAYER + CELLS] = jnp.broadcast_to(told[27:28], (8, CELLS))

    for copy in marks:
        copy.wait()
    _, prev_cell = places(count, before, prev_p[...], prev_o[...])
    _, next_cell = places(count, after, next_p[...], next_o[...])
    prev_cell = jnp.where(place > 0, prev_cell, -1)
    next_cell = jnp.where(place < count - 1, next_cell, -1)
    edges[...] = jnp.zeros_like(edges)
    edges[0:1, 0:HALF] = prev_cell.astype(F32)
    edges[0:1, HALF:V] = next_cell.astype(F32)
    fill_hot(prev_hot, prev_cell, 3 * LAYER)
    fill_hot(next_hot, next_cell, 0)
    for copy in halos:
        copy.wait()
    row = lax.broadcasted_iota(jnp.int32, (16, HALF), 0)
    half_lane = lax.broadcasted_iota(jnp.int32, (16, HALF), 1)
    for edge, where_hot, names, at in (
        (prev_f, prev_hot, EMPTY - HALF - half_lane, 0),
        (next_f, next_hot, V - half_lane, LAYER + CELLS),
    ):
        high, low = pieces(names)
        tail = jnp.where(row == 0, high, jnp.where(row == 1, low, 0.0)).astype(BF16)
        placed = dot_nt(jnp.concatenate([edge[...], tail], axis=0), where_hot[...])
        wide[:, at : at + LAYER] = placed[0:C].astype(BF16)
        ids[:, at : at + LAYER] = jnp.broadcast_to(
            placed[C : C + 1] * 64.0 + placed[C + 1 : C + 2], (8, LAYER)
        )

    for tap in range(9):
        seen[tap * 8 : (tap + 1) * 8, :] = shifted(ids[...], tap, masks)
    row = lax.broadcasted_iota(jnp.int32, (8, CELLS), 0)
    worst = jnp.zeros((8, CELLS), F32)
    for group in range(4):
        expect = jnp.zeros((8, CELLS), F32)
        for k in range(group * 8, min(group * 8 + 8, 27)):
            layer, tap = k // 9, k % 9
            expect = jnp.where(
                row == k % 8, seen[tap * 8 : (tap + 1) * 8, layer * LAYER : layer * LAYER + CELLS], expect
            )
        differs = jnp.abs(told[group * 8 : group * 8 + 8] - expect)
        if group == 3:
            differs = jnp.where(row < 3, differs, 0.0)
        worst = jnp.maximum(worst, differs)
    worst = jnp.where(jnp.broadcast_to(occupied, (8, CELLS)), worst, 0.0)
    wrong[0] = jnp.maximum(jnp.max(worst), jnp.max(-cell.astype(F32)))

    unfold(wide, masks, taps)
    weights = jnp.concatenate([w_conv[:, d * TAPS : (d + 1) * TAPS] for d in range(3)], axis=0)
    spread[...] = dot(weights, taps[...])

    coarse_halo.wait()
    lookup[0:128, :] = prev_g[128:VC, :]
    lookup[128:VC, :] = grads[0:128, :]
    product = dot_nt(w_down[...], lookup[...])
    blocks = []
    for b in range(8):
        h, at = b // 2 % 2, b // 4 * 128 + b % 2 * C
        blocks.append(
            jnp.concatenate(
                [product[(h * 4 + q) * C : (h * 4 + q + 1) * C, at : at + C] for q in range(4)], axis=1
            )
        )
    high, low = split(jnp.concatenate(blocks, axis=0))
    spread_back = octant_order(True)
    rows = dot(high, spread_back) + dot(low, spread_back)
    for b in range(8):
        back[:, b * 256 : (b + 1) * 256] = rows[b * C : (b + 1) * C]

    middles = []
    for b in range(8):
        at = b * 256
        act = (
            spread[0:C, at : at + 256]
            + spread[C : 2 * C, LAYER + at : LAYER + at + 256]
            + spread[2 * C : 3 * C, 2 * LAYER + at : 2 * LAYER + at + 256]
        )
        here = jnp.broadcast_to(occupied[:, at : at + 256], (C, 256))
        gate = jax.nn.sigmoid(act)
        held = wide[:, LAYER + at : LAYER + at + 256].astype(F32)
        middles.append(jnp.where(here, held + act * gate, 0.0).astype(BF16))
        slope = back[:, at : at + 256] * gate * (1.0 + act * (1.0 - gate))
        slopes[:, at : at + 256] = jnp.where(here, slope, 0.0).astype(BF16)

    sorted_ = dot(jnp.concatenate(middles, axis=0), octant_order(False)).astype(BF16)
    children = jnp.concatenate(
        [
            jnp.concatenate(
                [
                    sorted_[b * C : (b + 1) * C, q * C : (q + 1) * C]
                    for b in (2 * h, 2 * h + 1, 4 + 2 * h, 5 + 2 * h)
                ],
                axis=1,
            )
            for h in range(2)
            for q in range(4)
        ],
        axis=0,
    )
    sums = dot_tn(children, w_down[...])
    coarse_prev[0:128, :] = jnp.zeros((128, C2), BF16)
    coarse_prev[128:VC, :] = sums[0:128].astype(BF16)
    coarse_own[0:128, :] = sums[128:VC]
    coarse_own[128:VC, :] = jnp.zeros((128, C2), F32)
    part_b[128:ROWS_B, :] = dot(children, lookup[...])

    turned = slopes[...].T
    stack[...] = jnp.zeros_like(stack)
    for d in range(3):
        stack[d * LAYER : d * LAYER + CELLS, d * C : (d + 1) * C] = turned
    product = dot(taps[...], stack[...])
    conv[:, 27 * C : 28 * C] = jnp.zeros((C, C), F32)
    conv[:, 0 : 27 * C] = jnp.concatenate([product[:, d * C : (d + 1) * C].T for d in range(3)], axis=1)
    store_conv(conv, part_a, part_b)
    grad_pre[...] = dot(slopes[...], own_hot[...]).astype(BF16)


def repair_kernel(
    wrong, feats, prev_f, next_f, table, nbr, w_conv, w_down, grads, prev_g,
    old_pre, old_a, old_b, old_own, old_prev,
    grad_pre, part_a, part_b, coarse_own, coarse_prev, back,
    feats_v, cand, table_v, nbr_v, conv_v, down_v, lookup, rows, preact, slope_v, back_v, conv, spread, parent_hot,
    part_a_v, part_b_v, own_v, prev_v,
):
    @pl.when(wrong[0] > 0.0)
    def _():
        for src, dst in (
            (feats, feats_v), (prev_f, cand.at[:, pl.ds(0, HALF)]), (feats, cand.at[:, pl.ds(HALF, V)]),
            (next_f, cand.at[:, pl.ds(HALF + V, HALF)]), (table, table_v), (nbr, nbr_v), (w_conv, conv_v),
            (w_down, down_v), (prev_g, lookup.at[pl.ds(0, VC)]), (grads, lookup.at[pl.ds(VC, VC)]),
        ):
            pltpu.sync_copy(src, dst)
        preact[...] = dot(conv_v[:, 26 * C : 27 * C], named_rows(nbr_v[26:27, :], rows, cand[...]))

        def forward(i, carry):
            block = conv_v[:, pl.ds(pl.multiple_of(i * 128, 128), 128)]
            for half in range(2):
                read = named_rows(nbr_v[pl.ds(2 * i + half, 1), :], rows, cand[...])
                preact[...] += dot(block[:, half * C : (half + 1) * C], read)
            return carry

        lax.fori_loop(0, 13, forward, 0)
        act = preact[...]
        gate = jax.nn.sigmoid(act)
        middle = feats_v[...].astype(F32) + act * gate
        fill_hot(parent_hot, table_v[1:2, :].astype(jnp.int32), 0)
        parent_grads = dot_tn(lookup[...], parent_hot[...]).astype(BF16)
        back_all = dot(down_v[...], parent_grads)
        octant = table_v[2:3, :]
        total = jnp.zeros((C, V), F32)
        for o in range(8):
            chosen = jnp.broadcast_to(octant == float(o), (C, V))
            total += jnp.where(chosen, back_all[o * C : (o + 1) * C], 0.0)
            spread[o * C : (o + 1) * C, :] = jnp.where(chosen, middle, 0.0).astype(BF16)
        back_v[...] = total
        children = dot_nt(spread[...], parent_hot[...]).astype(BF16)
        sums = dot_tn(children, down_v[...])
        prev_v[...] = sums[0:VC].astype(BF16)
        own_v[...] = sums[VC : 2 * VC]
        part_b_v[128:ROWS_B, :] = dot(children, lookup[...])
        slope_v[...] = (total * gate * (1.0 + act * (1.0 - gate))).astype(BF16)

        def weight(i, carry):
            both = [
                dot_nt(slope_v[...], named_rows(nbr_v[pl.ds(2 * i + half, 1), :], rows, cand[...]))
                for half in range(2)
            ]
            conv[:, pl.ds(pl.multiple_of(i * 128, 128), 128)] = jnp.concatenate(both, axis=1)
            return carry

        lax.fori_loop(0, 13, weight, 0)
        last = dot_nt(slope_v[...], named_rows(nbr_v[26:27, :], rows, cand[...]))
        conv[:, 26 * C : 28 * C] = jnp.concatenate([last, jnp.zeros_like(last)], axis=1)
        store_conv(conv, part_a_v, part_b_v)
        for src, dst in (
            (slope_v, grad_pre), (part_a_v, part_a), (part_b_v, part_b), (own_v, coarse_own),
            (prev_v, coarse_prev), (back_v, back),
        ):
            pltpu.sync_copy(src, dst)


def total_kernel(
    count, dims, grad_pre, slopes, back, coarse_own, coarse, table, edges, w_conv, part_a, part_b,
    prev_p, next_p, coarse_out, grad_feats, done,
    got_a1, got_b1, sum_a1, sum_b1, got_a2, got_b2, got_z, coarse_in,
    own_hot, prev_hot, next_hot, wide, taps, weights, spread,
    halo_send, halo_recv, send_a, recv_a, send_b, recv_b, send_z, recv_z, send_g, recv_g,
):
    nx, nz, ny = dims
    place = lax.axis_index("space")
    y, z, x = place % ny, place // ny % nz, place // (ny * nz)
    after, before = (place + 1) % count, (place + count - 1) % count
    ys = [peer(place, dims, "y", d) for d in range(1, ny)]
    xs = [peer(place, dims, "x", d) for d in range(1, nx)]
    zs = [peer(place, dims, "z", d) for d in range(1, nz)]
    partners = [after, before] + ys + xs + zs
    signal(partners)

    fill_hot(own_hot, table[0:1, :].astype(jnp.int32), 0)
    fill_hot(prev_hot, edges[0:1, 0:HALF].astype(jnp.int32), 3 * LAYER)
    fill_hot(next_hot, edges[0:1, HALF:V].astype(jnp.int32), 0)
    await_partners(partners)

    first = []
    for d in range(1, ny):
        first.append(
            push(part_a.at[(y + d) % ny], got_a1.at[d - 1], send_a.at[0, d - 1], recv_a.at[0, d - 1], ys[d - 1])
        )
    for d in range(1, nx):
        first.append(
            push(part_b.at[(x + d) % nx], got_b1.at[d - 1], send_b.at[0, d - 1], recv_b.at[0, d - 1], xs[d - 1])
        )
    halos = [
        push(grad_pre.at[:, pl.ds(HALF, HALF)], prev_p, halo_send.at[0], halo_recv.at[0], after),
        push(grad_pre.at[:, pl.ds(0, HALF)], next_p, halo_send.at[1], halo_recv.at[1], before),
        push(coarse, coarse_in, halo_send.at[2], halo_recv.at[2], before),
    ]

    for layer in range(3):
        for tap in range(9):
            k = 26 - (layer * 9 + tap)
            weights[tap * C : (tap + 1) * C, layer * C : (layer + 1) * C] = w_conv[:, k * C : (k + 1) * C]

    for copy in first:
        copy.wait()
    size_a, size_b = ROWS_A // (ny * nx), ROWS_B // (ny * nx)
    total = part_a[y]
    for d in range(ny - 1):
        total += got_a1[d]
    for i in range(nx):
        sum_a1[i] = total[i * size_a : (i + 1) * size_a]
    total = part_b[x]
    for d in range(nx - 1):
        total += got_b1[d]
    for i in range(ny):
        sum_b1[i] = total[i * size_b : (i + 1) * size_b]
    second = []
    for d in range(1, nx):
        second.append(
            push(sum_a1.at[(x + d) % nx], got_a2.at[d - 1], send_a.at[1, d - 1], recv_a.at[1, d - 1], xs[d - 1])
        )
    for d in range(1, ny):
        second.append(
            push(sum_b1.at[(y + d) % ny], got_b2.at[d - 1], send_b.at[1, d - 1], recv_b.at[1, d - 1], ys[d - 1])
        )

    for copy in halos:
        copy.wait()
    coarse_out[...] = (coarse_own[...] + coarse_in[...].astype(F32)).astype(BF16)
    wide[:, 0:LAYER] = dot_nt(prev_p[...], prev_hot[...]).astype(BF16)
    wide[:, LAYER : LAYER + CELLS] = slopes[...]
    wide[:, LAYER + CELLS : WIDE] = dot_nt(next_p[...], next_hot[...]).astype(BF16)
    unfold(wide, edge_masks(), taps)

    for copy in second:
        copy.wait()
    total = sum_a1[x]
    for d in range(nx - 1):
        total += got_a2[d]
    got_z[z, 0:size_a, :] = total
    total = sum_b1[y]
    for d in range(ny - 1):
        total += got_b2[d]
    got_z[z, size_a : size_a + size_b, :] = total

    third = [
        push(got_z.at[z], got_z.at[z], send_z.at[d - 1], recv_z.at[d - 1], zs[d - 1])
        for d in range(1, nz)
    ]

    spread[...] = dot_tn(weights[...], taps[...])
    cells = (
        spread[0:C, 0:CELLS]
        + spread[C : 2 * C, LAYER : LAYER + CELLS]
        + spread[2 * C : 3 * C, 2 * LAYER : 2 * LAYER + CELLS]
        + back[...]
    )
    both = dot(jnp.concatenate(split(cells), axis=0), own_hot[...])
    grad_feats[...] = (both[0:C] + both[C : 2 * C]).astype(BF16)

    for copy in third:
        copy.wait()
    total = got_z[0]
    for i in range(1, nz):
        total += got_z[i]
    done[x, y, 0, 0:size_a, :] = total[0:size_a].astype(BF16)
    done[x, y, 1, 0:size_b, :] = total[size_a : size_a + size_b].astype(BF16)

    fourth = [
        push(done.at[x, y, 0], done.at[x, y, 0], send_g.at[0, d - 1], recv_g.at[0, d - 1], xs[d - 1])
        for d in range(1, nx)
    ] + [
        push(done.at[x, y, 1], done.at[x, y, 1], send_g.at[1, d - 1], recv_g.at[1, d - 1], ys[d - 1])
        for d in range(1, ny)
    ]
    for copy in fourth:
        copy.wait()
    fifth = [
        push(done.at[:, y, 0], done.at[:, y, 0], send_g.at[2, d - 1], recv_g.at[2, d - 1], ys[d - 1])
        for d in range(1, ny)
    ] + [
        push(done.at[x, :, 1], done.at[x, :, 1], send_g.at[3, d - 1], recv_g.at[3, d - 1], xs[d - 1])
        for d in range(1, nx)
    ]
    for copy in fifth:
        copy.wait()


def finish_kernel(
    dims, scale, wrong, grad_fast, coarse, done, grad_pre, prev_p, next_p, nbr, w_conv, back,
    coarse_out, grad_feats, grad_conv, grad_down,
    flat, cand, nbr_v, conv_v, spill, rows,
):
    nx, _, ny = dims
    coarse_out[...] = coarse[...]
    grad_feats[...] = grad_fast[...]
    size_a, size_b = ROWS_A // (ny * nx), ROWS_B // (ny * nx)
    for i in range(nx):
        for j in range(ny):
            at = (j * nx + i) * size_a
            flat[at : at + size_a, :] = done[i, j, 0, 0:size_a, :].astype(F32) * scale
            at = ROWS_A + (i * ny + j) * size_b
            flat[at : at + size_b, :] = done[i, j, 1, 0:size_b, :].astype(F32) * scale
    for t in range(13):
        grad_conv[:, t * 128 : (t + 1) * 128] = flat[t * C : (t + 1) * C, :]
    grad_conv[:, 13 * 128 : 27 * C] = flat[13 * C : 14 * C, 0:C]
    grad_down[...] = flat[14 * C : 14 * C + 8 * C, :]

    @pl.when(wrong[0] > 0.0)
    def _():
        for src, dst in (
            (prev_p, cand.at[:, pl.ds(0, HALF)]), (grad_pre, cand.at[:, pl.ds(HALF, V)]),
            (next_p, cand.at[:, pl.ds(HALF + V, HALF)]), (nbr, nbr_v), (w_conv, conv_v), (back, spill),
        ):
            pltpu.sync_copy(src, dst)
        spill[...] += dot_tn(conv_v[:, 26 * C : 27 * C], named_rows(nbr_v[0:1, :], rows, cand[...]))

        def pull(i, carry):
            block = conv_v[:, pl.ds(pl.multiple_of(i * 128, 128), 128)]
            for half in range(2):
                read = named_rows(nbr_v[pl.ds(26 - 2 * i - half, 1), :], rows, cand[...])
                spill[...] += dot_tn(block[:, half * C : (half + 1) * C], read)
            return carry

        lax.fori_loop(0, 13, pull, 0)
        grad_feats[...] = spill[...].astype(BF16)


def vmem(n):
    return [pl.BlockSpec(memory_space=pltpu.VMEM)] * n


def anywhere(n):
    return [pl.BlockSpec(memory_space=pl.ANY)] * n


def shape(dims, dtype):
    return jax.ShapeDtypeStruct(dims, dtype)


GRANT = 32 * 1024 * 1024


def per_device(feats, w_conv, w_down, neighbors, parent, octant, grad_out):
    count = lax.axis_size("space")
    dims = CHIPS[count]
    nx, nz, ny = dims
    feats, w_conv = feats.T, w_conv.T
    weights = w_conv
    feats, parent, octant, neighbors, w_conv, w_down, grad_out = (
        pltpu.with_memory_space_constraint(x, pltpu.HBM)
        for x in (
            feats, parent.reshape(1, V), octant.reshape(1, V), neighbors, w_conv, w_down, grad_out,
        )
    )
    dma = pltpu.SemaphoreType.DMA
    smem = [pl.BlockSpec(memory_space=pltpu.SMEM)]
    maps = [
        pltpu.VMEM((CELLS, V), BF16), pltpu.VMEM((LAYER, HALF), BF16), pltpu.VMEM((LAYER, HALF), BF16),
    ]
    half, row_half = shape((C, HALF), BF16), pltpu.VMEM((1, HALF), jnp.int32)

    (
        grad_pre, slopes, back, part_a, part_b, coarse_own, coarse_prev, wrong, table, edges,
        prev_f, next_f, prev_g,
    ) = pl.pallas_call(
        functools.partial(block_kernel, count),
        name="block",
        out_shape=(
            shape((C, V), BF16), shape((C, CELLS), BF16), shape((C, CELLS), F32),
            shape((ROWS_A, C2), F32), shape((ROWS_B, C2), F32), shape((VC, C2), F32), shape((VC, C2), BF16),
            shape((1,), F32), shape((8, V), F32), shape((8, V), F32), half, half, shape((VC, C2), BF16),
        ),
        in_specs=[pl.BlockSpec(memory_space=pltpu.HBM)] * 7,
        out_specs=tuple(vmem(7) + smem + vmem(5)),
        scratch_shapes=[row_half] * 4
        + maps
        + [
            pltpu.VMEM((C, WIDE), BF16), pltpu.VMEM((8, WIDE), F32), pltpu.VMEM((72, WIDE), F32),
            pltpu.VMEM((TAPS, WIDE), BF16), pltpu.VMEM((WIDE, 3 * C), BF16), pltpu.VMEM((32, V), jnp.int32),
            pltpu.VMEM((C, 28 * C), F32), pltpu.VMEM((3 * C, WIDE), F32), pltpu.VMEM((VC, C2), BF16),
            pltpu.VMEM((C, V), BF16), pltpu.VMEM((1, V), jnp.int32), pltpu.VMEM((1, V), jnp.int32),
            pltpu.VMEM((27, V), jnp.int32), pltpu.VMEM((C, 27 * C), BF16), pltpu.VMEM((8 * C, C2), BF16),
            pltpu.VMEM((VC, C2), BF16),
            dma((7,)), dma((7,)), dma((7,)),
        ],
        compiler_params=pltpu.CompilerParams(
            collective_id=0, has_side_effects=True, vmem_limit_bytes=GRANT
        ),
    )(feats, parent, octant, neighbors, w_conv, w_down, grad_out)

    grad_pre, part_a, part_b, coarse_own, coarse_prev, back_general = pl.pallas_call(
        repair_kernel,
        name="repair",
        out_shape=(
            shape((C, V), BF16), shape((ROWS_A, C2), F32), shape((ROWS_B, C2), F32),
            shape((VC, C2), F32), shape((VC, C2), BF16), shape((C, V), F32),
        ),
        in_specs=smem + anywhere(14),
        out_specs=tuple(anywhere(6)),
        input_output_aliases={10: 0, 11: 1, 12: 2, 13: 3, 14: 4},
        scratch_shapes=[
            pltpu.VMEM((C, V), BF16), pltpu.VMEM((C, 2 * V), BF16), pltpu.VMEM((8, V), F32),
            pltpu.VMEM((27, V), jnp.int32), pltpu.VMEM((C, 27 * C), BF16), pltpu.VMEM((8 * C, C2), BF16),
            pltpu.VMEM((2 * VC, C2), BF16), pltpu.VMEM((CELLS, V), BF16), pltpu.VMEM((C, V), F32),
            pltpu.VMEM((C, V), BF16), pltpu.VMEM((C, V), F32), pltpu.VMEM((C, 28 * C), F32),
            pltpu.VMEM((8 * C, V), BF16), pltpu.VMEM((2 * VC, V), BF16),
            pltpu.VMEM((ROWS_A, C2), F32), pltpu.VMEM((ROWS_B, C2), F32), pltpu.VMEM((VC, C2), F32),
            pltpu.VMEM((VC, C2), BF16),
        ],
        compiler_params=pltpu.CompilerParams(vmem_limit_bytes=GRANT),
    )(
        wrong, feats, prev_f, next_f, table, neighbors, w_conv, w_down, grad_out, prev_g,
        grad_pre, part_a, part_b, coarse_own, coarse_prev,
    )

    size_a, size_b = ROWS_A // (nx * ny), ROWS_B // (nx * ny)
    most = max(nx, ny) - 1
    prev_p, next_p, coarse_out, grad_feats, done = pl.pallas_call(
        functools.partial(total_kernel, count, dims),
        name="total",
        out_shape=(
            half, half, shape((VC, C2), BF16), shape((C, V), BF16), shape((nx, ny, 2, size_a, C2), BF16),
        ),
        in_specs=vmem(10),
        out_specs=tuple(vmem(5)),
        scratch_shapes=[
            pltpu.VMEM((ny - 1, ROWS_A // ny, C2), F32), pltpu.VMEM((nx - 1, ROWS_B // nx, C2), F32),
            pltpu.VMEM((nx, size_a, C2), F32), pltpu.VMEM((ny, size_b, C2), F32),
            pltpu.VMEM((nx - 1, size_a, C2), F32), pltpu.VMEM((ny - 1, size_b, C2), F32),
            pltpu.VMEM((nz, size_a + size_b, C2), F32), pltpu.VMEM((VC, C2), BF16),
        ]
        + maps
        + [
            pltpu.VMEM((C, WIDE), BF16), pltpu.VMEM((TAPS, WIDE), BF16), pltpu.VMEM((TAPS, 3 * C), BF16),
            pltpu.VMEM((3 * C, WIDE), F32),
            dma((3,)), dma((3,)), dma((2, most)), dma((2, most)), dma((2, most)), dma((2, most)),
            dma((nz - 1,)), dma((nz - 1,)), dma((4, most)), dma((4, most)),
        ],
        compiler_params=pltpu.CompilerParams(
            collective_id=1, has_side_effects=True, vmem_limit_bytes=GRANT
        ),
    )(
        grad_pre, slopes, back, coarse_own, coarse_prev, table, edges, weights,
        part_a.reshape(ny, ROWS_A // ny, C2), part_b.reshape(nx, ROWS_B // nx, C2),
    )

    coarse_out, grad_feats, grad_conv, grad_down = pl.pallas_call(
        functools.partial(finish_kernel, dims, 1.0 / math.sqrt(V * count)),
        name="finish",
        out_shape=(
            shape((VC, C2), BF16), shape((C, V), BF16), shape((C, 27 * C), F32), shape((8 * C, C2), F32),
        ),
        in_specs=smem + vmem(3) + anywhere(6),
        out_specs=tuple(vmem(4)),
        scratch_shapes=[
            pltpu.VMEM((ROWS_A + ROWS_B, C2), F32), pltpu.VMEM((C, 2 * V), BF16),
            pltpu.VMEM((27, V), jnp.int32), pltpu.VMEM((C, 27 * C), BF16), pltpu.VMEM((C, V), F32),
            pltpu.VMEM((CELLS, V), BF16),
        ],
        compiler_params=pltpu.CompilerParams(vmem_limit_bytes=GRANT),
    )(
        wrong, grad_feats, coarse_out, done, grad_pre, prev_p, next_p, neighbors, w_conv, back_general,
    )
    return coarse_out, grad_feats.T, grad_conv.T, grad_down


def solution(mesh):
    rows = P(("dp", "space"), None)
    line = P(("dp", "space"))
    return jax.shard_map(
        per_device,
        mesh=mesh,
        in_specs=(rows, P(), P(), P(None, ("dp", "space")), line, line, rows),
        out_specs=(rows, rows, P("dp", None), P("dp", None)),
        check_vma=False,
    )
```

```python
import functools
import math

import jax
import jax.numpy as jnp
from jax import lax
from jax.experimental import pallas as pl
from jax.experimental.pallas import tpu as pltpu
from jax.sharding import PartitionSpec as P

F32 = jnp.float32
BF16 = jnp.bfloat16
C = 64
C2 = 128
V = 1024
HALF = 512
VC = 256
SY, SZ = 32, 16
LAYER = SY * SZ
CELLS = 4 * LAYER
WIDE = CELLS + 2 * LAYER
EMPTY = 3 * V
TAPS = 9 * C
SUMS = 22 * C
CHUNK = 96
CHIPS = {128: (4, 8, 4)}


def dot(a, b):
    return jnp.dot(a, b, preferred_element_type=F32)


def dot_nt(a, b):
    return lax.dot_general(a, b, (((1,), (1,)), ((), ())), preferred_element_type=F32)


def dot_tn(a, b):
    return lax.dot_general(a, b, (((0,), (0,)), ((), ())), preferred_element_type=F32)


def fill_hot(ref, ids, first):
    high = jnp.broadcast_to(
        lax.shift_right_arithmetic(ids, 4).astype(F32).astype(BF16), (16, ids.shape[1])
    )
    row = lax.broadcasted_iota(jnp.int32, high.shape, 0)
    low = jnp.where(row == (ids & 15), 1.0, 0.0).astype(BF16)
    none = jnp.zeros_like(low)
    for t in range(ref.shape[0] // 16):
        ref[t * 16 : (t + 1) * 16, :] = jnp.where(
            high == jnp.asarray(first // 16 + t, BF16), low, none
        )


def fill_hot_t(ref, ids, first):
    count = ids.shape[1]
    high, low = lax.shift_right_arithmetic(ids, 7).astype(F32), (ids & 127).astype(F32)
    row = lax.broadcasted_iota(jnp.int32, (8, count), 0)
    columns = jnp.where(row == 0, jnp.broadcast_to(high, row.shape), jnp.broadcast_to(low, row.shape)).T
    lane = lax.broadcasted_iota(jnp.int32, (count, 128), 1).astype(F32)
    high = jnp.broadcast_to(columns[:, 0:1], lane.shape).astype(BF16)
    low = jnp.where(jnp.broadcast_to(columns[:, 1:2], lane.shape) == lane, 1.0, 0.0).astype(BF16)
    none = jnp.zeros_like(low)
    for t in range(ref.shape[1] // 128):
        ref[:, t * 128 : (t + 1) * 128] = jnp.where(
            high == jnp.asarray(first // 128 + t, BF16), low, none
        )


def peer(place, dims, axis, step):
    _, nz, ny = dims
    y, z, x = place % ny, place // ny % nz, place // (ny * nz)
    if axis == "y":
        return place - y + (y + step) % ny
    if axis == "z":
        return place + ((z + step) % nz - z) * ny
    return place + ((x + step) % dims[0] - x) * (ny * nz)


def signal(partners):
    barrier = pltpu.get_barrier_semaphore()
    for other in partners:
        pl.semaphore_signal(
            barrier, inc=1, device_id={"space": other}, device_id_type=pl.DeviceIdType.MESH
        )


def await_partners(partners):
    pl.semaphore_wait(pltpu.get_barrier_semaphore(), len(partners))


def push(src, dst, send, recv, other):
    copy = pltpu.make_async_remote_copy(
        src_ref=src,
        dst_ref=dst,
        send_sem=send,
        recv_sem=recv,
        device_id={"space": other},
        device_id_type=pl.DeviceIdType.MESH,
    )
    copy.start()
    return copy


def places(count, place, parent, octant):
    own, prev = place * VC, (place + count - 1) % count * VC
    inside = (parent >= own) & (parent < own + VC)
    coarse = jnp.where(inside, parent - own + VC, parent - prev)
    layer = lax.shift_right_arithmetic(coarse, 7) - 1
    cell = (
        (2 * layer + lax.shift_right_arithmetic(octant, 2)) * LAYER
        + (2 * lax.shift_right_arithmetic(coarse & 127, 3) + (lax.shift_right_arithmetic(octant, 1) & 1)) * SZ
        + 2 * (coarse & 7)
        + (octant & 1)
    )
    return coarse, jnp.where((layer == 0) | (layer == 1), cell, -1)


def edge_masks():
    lane = lax.broadcasted_iota(jnp.int32, (1, LAYER), 1)
    y, z = lax.shift_right_arithmetic(lane, 4), lane & (SZ - 1)
    masks = []
    for dy in (-1, 0, 1):
        for dz in (-1, 0, 1):
            inside = (y + dy >= 0) & (y + dy < SY) & (z + dz >= 0) & (z + dz < SZ)
            masks.append(jnp.where(inside, 1.0, 0.0))
    return masks


def shifted(block, tap, masks):
    step = (tap // 3 - 1) * SZ + tap % 3 - 1
    if step == 0:
        return block
    rows = block.shape[0]
    mask = jnp.broadcast_to(masks[tap], (rows, LAYER)).astype(block.dtype)
    return pltpu.roll(block, (-step) % WIDE, 1) * jnp.concatenate([mask] * (WIDE // LAYER), axis=1)


def unfold(wide, masks, taps):
    for group in range(0, C, 16):
        block = wide[group : group + 16, :]
        for tap in range(9):
            taps[tap * C + group : tap * C + group + 16, :] = shifted(block, tap, masks)


def split(x):
    high = x.astype(BF16)
    return high, (x - high.astype(F32)).astype(BF16)


def named_rows(names, rows, candidates):
    fill_hot(rows, names, HALF)
    return dot(candidates, rows[...]).astype(BF16)


def pieces(ids):
    return lax.shift_right_logical(ids, 6).astype(F32), (ids & 63).astype(F32)


def octant_order(flip):
    shape_ = (256, 256)
    cell = lax.broadcasted_iota(jnp.int32, shape_, 1 if flip else 0)
    slot = lax.broadcasted_iota(jnp.int32, shape_, 0 if flip else 1)
    corner, pair = lax.shift_right_arithmetic(slot, 6), slot & 63
    y = 2 * lax.shift_right_arithmetic(pair, 3) + lax.shift_right_arithmetic(corner, 1)
    z = 2 * (pair & 7) + (corner & 1)
    return jnp.where(cell == y * SZ + z, 1.0, 0.0).astype(BF16)


def store_conv(conv, sums):
    for t in range(14):
        sums[t * C : (t + 1) * C, :] = conv[:, t * 128 : (t + 1) * 128].astype(BF16)
    sums[SUMS : sums.shape[0], :] = jnp.zeros((sums.shape[0] - SUMS, C2), BF16)


def block_kernel(
    count, feats_in, parent_in, octant_in, nbr_in, w_conv_in, w_down_in, grads_in,
    slopes, back, sums, coarse_own, coarse_prev, wrong, table, edges,
    prev_f, next_f, prev_g,
    prev_p, next_p, prev_o, next_o, own_hot, prev_hot, next_hot, wide, ids, seen, taps, stack, named,
    conv, spread, lookup, feats, parent, octant, nbr, w_conv, w_down, grads, send, recv, load,
):
    place = lax.axis_index("space")
    after, before = (place + 1) % count, (place + count - 1) % count
    signal((after, before))
    inputs = (
        (parent_in, parent), (octant_in, octant), (feats_in, feats), (grads_in, grads), (nbr_in, nbr),
        (w_conv_in, w_conv), (w_down_in, w_down),
    )
    loads = [pltpu.make_async_copy(src, dst, load.at[i]) for i, (src, dst) in enumerate(inputs)]
    for copy in loads:
        copy.start()
    for copy in loads[0:4]:
        copy.wait()
    await_partners((after, before))
    late, early = pl.ds(HALF, HALF), pl.ds(0, HALF)
    marks = [
        push(parent.at[:, late], prev_p, send.at[0], recv.at[0], after),
        push(octant.at[:, late], prev_o, send.at[1], recv.at[1], after),
        push(parent.at[:, early], next_p, send.at[2], recv.at[2], before),
        push(octant.at[:, early], next_o, send.at[3], recv.at[3], before),
    ]
    halos = [
        push(feats.at[:, late], prev_f, send.at[4], recv.at[4], after),
        push(feats.at[:, early], next_f, send.at[5], recv.at[5], before),
    ]
    coarse_halo = push(grads, prev_g, send.at[6], recv.at[6], after)

    for copy in loads[4:]:
        copy.wait()
    coarse, cell = places(count, place, parent[...], octant[...])
    table[...] = jnp.zeros_like(table)
    table[0:1, :] = cell.astype(F32)
    table[1:2, :] = coarse.astype(F32)
    table[2:3, :] = octant[...].astype(F32)
    fill_hot_t(own_hot, cell, 0)
    masks = edge_masks()
    lane = lax.broadcasted_iota(jnp.int32, (1, V), 1)
    named[...] = jnp.zeros_like(named)
    named[0:27, :] = EMPTY - nbr[...]
    named[27:28, :] = 2 * V - lane
    high, low = pieces(named[...])
    own = jnp.concatenate([feats[...], high.astype(BF16), low.astype(BF16)], axis=0)
    own = dot(own, own_hot[...])
    wide[:, LAYER : LAYER + CELLS] = own[0:C].astype(BF16)
    told = own[C : C + 32] * 64.0 + own[C + 32 : C + 64]
    occupied = told[27:28] > 0.0
    ids[:, LAYER : LAYER + CELLS] = jnp.broadcast_to(told[27:28], (8, CELLS))

    for copy in marks:
        copy.wait()
    _, prev_cell = places(count, before, prev_p[...], prev_o[...])
    _, next_cell = places(count, after, next_p[...], next_o[...])
    prev_cell = jnp.where(place > 0, prev_cell, -1)
    next_cell = jnp.where(place < count - 1, next_cell, -1)
    edges[...] = jnp.zeros_like(edges)
    edges[0:1, 0:HALF] = prev_cell.astype(F32)
    edges[0:1, HALF:V] = next_cell.astype(F32)
    fill_hot_t(prev_hot, prev_cell, 3 * LAYER)
    fill_hot_t(next_hot, next_cell, 0)
    for copy in halos:
        copy.wait()
    row = lax.broadcasted_iota(jnp.int32, (16, HALF), 0)
    half_lane = lax.broadcasted_iota(jnp.int32, (16, HALF), 1)
    for edge, where_hot, names, at in (
        (prev_f, prev_hot, EMPTY - HALF - half_lane, 0),
        (next_f, next_hot, V - half_lane, LAYER + CELLS),
    ):
        high, low = pieces(names)
        tail = jnp.where(row == 0, high, jnp.where(row == 1, low, 0.0)).astype(BF16)
        placed = dot(jnp.concatenate([edge[...], tail], axis=0), where_hot[...])
        wide[:, at : at + LAYER] = placed[0:C].astype(BF16)
        ids[:, at : at + LAYER] = jnp.broadcast_to(
            placed[C : C + 1] * 64.0 + placed[C + 1 : C + 2], (8, LAYER)
        )

    for tap in range(9):
        seen[tap * 8 : (tap + 1) * 8, :] = shifted(ids[...], tap, masks)
    row = lax.broadcasted_iota(jnp.int32, (8, CELLS), 0)
    worst = jnp.zeros((8, CELLS), F32)
    for group in range(4):
        expect = jnp.zeros((8, CELLS), F32)
        for k in range(group * 8, min(group * 8 + 8, 27)):
            layer, tap = k // 9, k % 9
            expect = jnp.where(
                row == k % 8, seen[tap * 8 : (tap + 1) * 8, layer * LAYER : layer * LAYER + CELLS], expect
            )
        differs = jnp.abs(told[group * 8 : group * 8 + 8] - expect)
        if group == 3:
            differs = jnp.where(row < 3, differs, 0.0)
        worst = jnp.maximum(worst, differs)
    worst = jnp.where(jnp.broadcast_to(occupied, (8, CELLS)), worst, 0.0)
    wrong[0] = jnp.maximum(jnp.max(worst), jnp.max(-cell.astype(F32)))

    unfold(wide, masks, taps)
    weights = jnp.concatenate([w_conv[:, d * TAPS : (d + 1) * TAPS] for d in range(3)], axis=0)
    spread[...] = dot(weights, taps[...])

    coarse_halo.wait()
    lookup[0:128, :] = prev_g[128:VC, :]
    lookup[128:VC, :] = grads[0:128, :]
    product = dot_nt(w_down[...], lookup[...])
    blocks = []
    for b in range(8):
        h, at = b // 2 % 2, b // 4 * 128 + b % 2 * C
        blocks.append(
            jnp.concatenate(
                [product[(h * 4 + q) * C : (h * 4 + q + 1) * C, at : at + C] for q in range(4)], axis=1
            )
        )
    high, low = split(jnp.concatenate(blocks, axis=0))
    spread_back = octant_order(True)
    rows = dot(high, spread_back) + dot(low, spread_back)
    for b in range(8):
        back[:, b * 256 : (b + 1) * 256] = rows[b * C : (b + 1) * C]

    middles = []
    for b in range(8):
        at = b * 256
        act = (
            spread[0:C, at : at + 256]
            + spread[C : 2 * C, LAYER + at : LAYER + at + 256]
            + spread[2 * C : 3 * C, 2 * LAYER + at : 2 * LAYER + at + 256]
        )
        here = jnp.broadcast_to(occupied[:, at : at + 256], (C, 256))
        gate = jax.nn.sigmoid(act)
        held = wide[:, LAYER + at : LAYER + at + 256].astype(F32)
        middles.append(jnp.where(here, held + act * gate, 0.0).astype(BF16))
        slope = back[:, at : at + 256] * gate * (1.0 + act * (1.0 - gate))
        slopes[:, at : at + 256] = jnp.where(here, slope, 0.0).astype(BF16)

    sorted_ = dot(jnp.concatenate(middles, axis=0), octant_order(False)).astype(BF16)
    children = jnp.concatenate(
        [
            jnp.concatenate(
                [
                    sorted_[b * C : (b + 1) * C, q * C : (q + 1) * C]
                    for b in (2 * h, 2 * h + 1, 4 + 2 * h, 5 + 2 * h)
                ],
                axis=1,
            )
            for h in range(2)
            for q in range(4)
        ],
        axis=0,
    )
    coarse = dot_tn(children, w_down[...])
    coarse_prev[0:128, :] = jnp.zeros((128, C2), BF16)
    coarse_prev[128:VC, :] = coarse[0:128].astype(BF16)
    coarse_own[0:128, :] = coarse[128:VC]
    coarse_own[128:VC, :] = jnp.zeros((128, C2), F32)
    sums[14 * C : SUMS, :] = dot(children, lookup[...]).astype(BF16)

    turned = slopes[...].T
    stack[...] = jnp.zeros_like(stack)
    for d in range(3):
        stack[d * LAYER : d * LAYER + CELLS, d * C : (d + 1) * C] = turned
    product = dot(taps[...], stack[...])
    conv[:, 27 * C : 28 * C] = jnp.zeros((C, C), F32)
    conv[:, 0 : 27 * C] = jnp.concatenate([product[:, d * C : (d + 1) * C].T for d in range(3)], axis=1)
    store_conv(conv, sums)


def repair_kernel(
    wrong, feats, prev_f, next_f, table, nbr, w_conv, w_down, grads, prev_g,
    old_sums, old_own, old_prev,
    sums, coarse_own, coarse_prev, grad_pre, back,
    feats_v, cand, table_v, nbr_v, conv_v, down_v, lookup, rows, preact, slope_v, back_v, conv, spread, parent_hot,
    sums_v, own_v, prev_v,
):
    @pl.when(wrong[0] > 0.0)
    def _():
        for src, dst in (
            (feats, feats_v), (prev_f, cand.at[:, pl.ds(0, HALF)]), (feats, cand.at[:, pl.ds(HALF, V)]),
            (next_f, cand.at[:, pl.ds(HALF + V, HALF)]), (table, table_v), (nbr, nbr_v), (w_conv, conv_v),
            (w_down, down_v), (prev_g, lookup.at[pl.ds(0, VC)]), (grads, lookup.at[pl.ds(VC, VC)]),
        ):
            pltpu.sync_copy(src, dst)
        preact[...] = dot(conv_v[:, 26 * C : 27 * C], named_rows(nbr_v[26:27, :], rows, cand[...]))

        def forward(i, carry):
            block = conv_v[:, pl.ds(pl.multiple_of(i * 128, 128), 128)]
            for half in range(2):
                read = named_rows(nbr_v[pl.ds(2 * i + half, 1), :], rows, cand[...])
                preact[...] += dot(block[:, half * C : (half + 1) * C], read)
            return carry

        lax.fori_loop(0, 13, forward, 0)
        act = preact[...]
        gate = jax.nn.sigmoid(act)
        middle = feats_v[...].astype(F32) + act * gate
        fill_hot(parent_hot, table_v[1:2, :].astype(jnp.int32), 0)
        parent_grads = dot_tn(lookup[...], parent_hot[...]).astype(BF16)
        back_all = dot(down_v[...], parent_grads)
        octant = table_v[2:3, :]
        total = jnp.zeros((C, V), F32)
        for o in range(8):
            chosen = jnp.broadcast_to(octant == float(o), (C, V))
            total += jnp.where(chosen, back_all[o * C : (o + 1) * C], 0.0)
            spread[o * C : (o + 1) * C, :] = jnp.where(chosen, middle, 0.0).astype(BF16)
        back_v[...] = total
        children = dot_nt(spread[...], parent_hot[...]).astype(BF16)
        coarse = dot_tn(children, down_v[...])
        prev_v[...] = coarse[0:VC].astype(BF16)
        own_v[...] = coarse[VC : 2 * VC]
        sums_v[14 * C : SUMS, :] = dot(children, lookup[...]).astype(BF16)
        slope_v[...] = (total * gate * (1.0 + act * (1.0 - gate))).astype(BF16)

        def weight(i, carry):
            both = [
                dot_nt(slope_v[...], named_rows(nbr_v[pl.ds(2 * i + half, 1), :], rows, cand[...]))
                for half in range(2)
            ]
            conv[:, pl.ds(pl.multiple_of(i * 128, 128), 128)] = jnp.concatenate(both, axis=1)
            return carry

        lax.fori_loop(0, 13, weight, 0)
        last = dot_nt(slope_v[...], named_rows(nbr_v[26:27, :], rows, cand[...]))
        conv[:, 26 * C : 28 * C] = jnp.concatenate([last, jnp.zeros_like(last)], axis=1)
        store_conv(conv, sums_v)
        for src, dst in (
            (slope_v, grad_pre), (sums_v, sums), (own_v, coarse_own), (prev_v, coarse_prev), (back_v, back),
        ):
            pltpu.sync_copy(src, dst)


def total_kernel(
    count, dims, wrong, general, slopes, back, coarse_own, coarse, table, edges, w_conv, sums,
    prev_p, next_p, coarse_out, grad_feats, done,
    got, got_z, coarse_in, grad_pre, own_hot, prev_hot, next_hot, wide, taps, weights, spread,
    halo_send, halo_recv, send, recv, send_z, recv_z, send_g, recv_g,
):
    nx, nz, ny = dims
    place = lax.axis_index("space")
    y, z, x = place % ny, place // ny % nz, place // (ny * nz)
    mine = x * ny + y
    after, before = (place + 1) % count, (place + count - 1) % count
    steps = [(dx, dy) for dx in range(nx) for dy in range(ny)][1:]
    plane = [peer(peer(place, dims, "x", dx), dims, "y", dy) for dx, dy in steps]
    column = [peer(place, dims, "z", d) for d in range(1, nz)]
    partners = [after, before] + plane + column
    signal(partners)

    fill_hot(own_hot, table[0:1, :].astype(jnp.int32), 0)
    fill_hot_t(prev_hot, edges[0:1, 0:HALF].astype(jnp.int32), 3 * LAYER)
    fill_hot_t(next_hot, edges[0:1, HALF:V].astype(jnp.int32), 0)
    await_partners(partners)

    first = [
        push(sums.at[(x + dx) % nx * ny + (y + dy) % ny], got.at[i], send.at[i], recv.at[i], plane[i])
        for i, (dx, dy) in enumerate(steps)
    ]

    fast = dot(slopes[...], own_hot[...])
    repaired = jnp.broadcast_to(wrong[0], fast.shape) > 0.0
    grad_pre[...] = jnp.where(repaired, general[...].astype(F32), fast).astype(BF16)
    for layer in range(3):
        for tap in range(9):
            k = 26 - (layer * 9 + tap)
            weights[tap * C : (tap + 1) * C, layer * C : (layer + 1) * C] = w_conv[:, k * C : (k + 1) * C]

    for copy in first:
        copy.wait()
    halos = [
        push(grad_pre.at[:, pl.ds(HALF, HALF)], prev_p, halo_send.at[0], halo_recv.at[0], after),
        push(grad_pre.at[:, pl.ds(0, HALF)], next_p, halo_send.at[1], halo_recv.at[1], before),
        push(coarse, coarse_in, halo_send.at[2], halo_recv.at[2], before),
    ]
    total = sums[mine].astype(F32)
    for i in range(len(steps)):
        total += got[i].astype(F32)
    got_z[z] = total.astype(BF16)

    second = [
        push(got_z.at[z], got_z.at[z], send_z.at[d - 1], recv_z.at[d - 1], column[d - 1])
        for d in range(1, nz)
    ]

    for copy in halos:
        copy.wait()
    coarse_out[...] = (coarse_own[...] + coarse_in[...].astype(F32)).astype(BF16)
    wide[:, 0:LAYER] = dot(prev_p[...], prev_hot[...]).astype(BF16)
    wide[:, LAYER : LAYER + CELLS] = slopes[...]
    wide[:, LAYER + CELLS : WIDE] = dot(next_p[...], next_hot[...]).astype(BF16)
    unfold(wide, edge_masks(), taps)

    for copy in second:
        copy.wait()
    total = got_z[0].astype(F32)
    for i in range(1, nz):
        total += got_z[i].astype(F32)
    done[mine] = total.astype(BF16)

    third = [
        push(done.at[mine], done.at[mine], send_g.at[i], recv_g.at[i], plane[i]) for i in range(len(steps))
    ]

    spread[...] = dot_tn(weights[...], taps[...])
    cells = (
        spread[0:C, 0:CELLS]
        + spread[C : 2 * C, LAYER : LAYER + CELLS]
        + spread[2 * C : 3 * C, 2 * LAYER : 2 * LAYER + CELLS]
        + back[...]
    )
    both = dot(jnp.concatenate(split(cells), axis=0), own_hot[...])
    grad_feats[...] = (both[0:C] + both[C : 2 * C]).astype(BF16)
    for copy in third:
        copy.wait()


def finish_kernel(
    scale, wrong, grad_fast, coarse, done, grad_pre, prev_p, next_p, nbr, w_conv, back,
    coarse_out, grad_feats, grad_conv, grad_down,
    cand, nbr_v, conv_v, spill, rows,
):
    coarse_out[...] = coarse[...]
    grad_feats[...] = grad_fast[...]
    for t in range(13):
        grad_conv[:, t * 128 : (t + 1) * 128] = done[t * C : (t + 1) * C, :].astype(F32) * scale
    grad_conv[:, 13 * 128 : 27 * C] = done[13 * C : 14 * C, 0:C].astype(F32) * scale
    grad_down[...] = done[14 * C : SUMS, :].astype(F32) * scale

    @pl.when(wrong[0] > 0.0)
    def _():
        for src, dst in (
            (prev_p, cand.at[:, pl.ds(0, HALF)]), (grad_pre, cand.at[:, pl.ds(HALF, V)]),
            (next_p, cand.at[:, pl.ds(HALF + V, HALF)]), (nbr, nbr_v), (w_conv, conv_v), (back, spill),
        ):
            pltpu.sync_copy(src, dst)
        spill[...] += dot_tn(conv_v[:, 26 * C : 27 * C], named_rows(nbr_v[0:1, :], rows, cand[...]))

        def pull(i, carry):
            block = conv_v[:, pl.ds(pl.multiple_of(i * 128, 128), 128)]
            for half in range(2):
                read = named_rows(nbr_v[pl.ds(26 - 2 * i - half, 1), :], rows, cand[...])
                spill[...] += dot_tn(block[:, half * C : (half + 1) * C], read)
            return carry

        lax.fori_loop(0, 13, pull, 0)
        grad_feats[...] = spill[...].astype(BF16)


def vmem(n):
    return [pl.BlockSpec(memory_space=pltpu.VMEM)] * n


def anywhere(n):
    return [pl.BlockSpec(memory_space=pl.ANY)] * n


def shape(dims, dtype):
    return jax.ShapeDtypeStruct(dims, dtype)


GRANT = 32 * 1024 * 1024


def per_device(feats, w_conv, w_down, neighbors, parent, octant, grad_out):
    count = lax.axis_size("space")
    dims = CHIPS[count]
    nx, nz, ny = dims
    feats, w_conv = feats.T, w_conv.T
    weights = w_conv
    feats, parent, octant, neighbors, w_conv, w_down, grad_out = (
        pltpu.with_memory_space_constraint(x, pltpu.HBM)
        for x in (
            feats, parent.reshape(1, V), octant.reshape(1, V), neighbors, w_conv, w_down, grad_out,
        )
    )
    dma = pltpu.SemaphoreType.DMA
    smem = [pl.BlockSpec(memory_space=pltpu.SMEM)]
    maps = [
        pltpu.VMEM((CELLS, V), BF16), pltpu.VMEM((LAYER, HALF), BF16), pltpu.VMEM((LAYER, HALF), BF16),
    ]
    maps_t = [pltpu.VMEM((V, CELLS), BF16)] + maps[1:]
    half, row_half = shape((C, HALF), BF16), pltpu.VMEM((1, HALF), jnp.int32)
    padded = shape((nx * ny * CHUNK, C2), BF16)

    (
        slopes, back, sums, coarse_own, coarse_prev, wrong, table, edges, prev_f, next_f, prev_g,
    ) = pl.pallas_call(
        functools.partial(block_kernel, count),
        name="block",
        out_shape=(
            shape((C, CELLS), BF16), shape((C, CELLS), F32), padded,
            shape((VC, C2), F32), shape((VC, C2), BF16),
            shape((1,), F32), shape((8, V), F32), shape((8, V), F32), half, half, shape((VC, C2), BF16),
        ),
        in_specs=[pl.BlockSpec(memory_space=pltpu.HBM)] * 7,
        out_specs=tuple(vmem(5) + smem + vmem(5)),
        scratch_shapes=[row_half] * 4
        + maps_t
        + [
            pltpu.VMEM((C, WIDE), BF16), pltpu.VMEM((8, WIDE), F32), pltpu.VMEM((72, WIDE), F32),
            pltpu.VMEM((TAPS, WIDE), BF16), pltpu.VMEM((WIDE, 3 * C), BF16), pltpu.VMEM((32, V), jnp.int32),
            pltpu.VMEM((C, 28 * C), F32), pltpu.VMEM((3 * C, WIDE), F32), pltpu.VMEM((VC, C2), BF16),
            pltpu.VMEM((C, V), BF16), pltpu.VMEM((1, V), jnp.int32), pltpu.VMEM((1, V), jnp.int32),
            pltpu.VMEM((27, V), jnp.int32), pltpu.VMEM((C, 27 * C), BF16), pltpu.VMEM((8 * C, C2), BF16),
            pltpu.VMEM((VC, C2), BF16),
            dma((7,)), dma((7,)), dma((7,)),
        ],
        compiler_params=pltpu.CompilerParams(
            collective_id=0, has_side_effects=True, vmem_limit_bytes=GRANT
        ),
    )(feats, parent, octant, neighbors, w_conv, w_down, grad_out)

    sums, coarse_own, coarse_prev, general, back_general = pl.pallas_call(
        repair_kernel,
        name="repair",
        out_shape=(
            padded, shape((VC, C2), F32), shape((VC, C2), BF16), shape((C, V), BF16), shape((C, V), F32),
        ),
        in_specs=smem + anywhere(12),
        out_specs=tuple(anywhere(5)),
        input_output_aliases={10: 0, 11: 1, 12: 2},
        scratch_shapes=[
            pltpu.VMEM((C, V), BF16), pltpu.VMEM((C, 2 * V), BF16), pltpu.VMEM((8, V), F32),
            pltpu.VMEM((27, V), jnp.int32), pltpu.VMEM((C, 27 * C), BF16), pltpu.VMEM((8 * C, C2), BF16),
            pltpu.VMEM((2 * VC, C2), BF16), pltpu.VMEM((CELLS, V), BF16), pltpu.VMEM((C, V), F32),
            pltpu.VMEM((C, V), BF16), pltpu.VMEM((C, V), F32), pltpu.VMEM((C, 28 * C), F32),
            pltpu.VMEM((8 * C, V), BF16), pltpu.VMEM((2 * VC, V), BF16),
            pltpu.VMEM(padded.shape, BF16), pltpu.VMEM((VC, C2), F32), pltpu.VMEM((VC, C2), BF16),
        ],
        compiler_params=pltpu.CompilerParams(vmem_limit_bytes=GRANT),
    )(
        wrong, feats, prev_f, next_f, table, neighbors, w_conv, w_down, grad_out, prev_g,
        sums, coarse_own, coarse_prev,
    )

    chunks, others = (nx * ny, CHUNK, C2), nx * ny - 1
    prev_p, next_p, coarse_out, grad_feats, done = pl.pallas_call(
        functools.partial(total_kernel, count, dims),
        name="total",
        out_shape=(
            half, half, shape((VC, C2), BF16), shape((C, V), BF16), shape(chunks, BF16),
        ),
        in_specs=smem + vmem(9),
        out_specs=tuple(vmem(5)),
        scratch_shapes=[
            pltpu.VMEM((others, CHUNK, C2), BF16), pltpu.VMEM((nz, CHUNK, C2), BF16),
            pltpu.VMEM((VC, C2), BF16), pltpu.VMEM((C, V), BF16),
        ]
        + maps
        + [
            pltpu.VMEM((C, WIDE), BF16), pltpu.VMEM((TAPS, WIDE), BF16), pltpu.VMEM((TAPS, 3 * C), BF16),
            pltpu.VMEM((3 * C, WIDE), F32),
            dma((3,)), dma((3,)), dma((others,)), dma((others,)), dma((nz - 1,)), dma((nz - 1,)),
            dma((others,)), dma((others,)),
        ],
        compiler_params=pltpu.CompilerParams(
            collective_id=1, has_side_effects=True, vmem_limit_bytes=GRANT
        ),
    )(
        wrong, general, slopes, back, coarse_own, coarse_prev, table, edges, weights, sums.reshape(chunks),
    )

    coarse_out, grad_feats, grad_conv, grad_down = pl.pallas_call(
        functools.partial(finish_kernel, 1.0 / math.sqrt(V * count)),
        name="finish",
        out_shape=(
            shape((VC, C2), BF16), shape((C, V), BF16), shape((C, 27 * C), F32), shape((8 * C, C2), F32),
        ),
        in_specs=smem + vmem(3) + anywhere(6),
        out_specs=tuple(vmem(4)),
        scratch_shapes=[
            pltpu.VMEM((C, 2 * V), BF16),
            pltpu.VMEM((27, V), jnp.int32), pltpu.VMEM((C, 27 * C), BF16), pltpu.VMEM((C, V), F32),
            pltpu.VMEM((CELLS, V), BF16),
        ],
        compiler_params=pltpu.CompilerParams(vmem_limit_bytes=GRANT),
    )(
        wrong, grad_feats, coarse_out, done.reshape(padded.shape), general, prev_p, next_p, neighbors, w_conv,
        back_general,
    )
    return coarse_out, grad_feats.T, grad_conv.T, grad_down


def solution(mesh):
    rows = P(("dp", "space"), None)
    line = P(("dp", "space"))
    return jax.shard_map(
        per_device,
        mesh=mesh,
        in_specs=(rows, P(), P(), P(None, ("dp", "space")), line, line, rows),
        out_specs=(rows, rows, P("dp", None), P("dp", None)),
        check_vma=False,
    )
```
